256 devices in a mesh: gx: 4 (over y), gy: 16 (over z, core), gz: 4 (over x).
Axes of the slice: x: 4, y: 4, z: 8, core: 2. Of those that a mesh axis runs over, the one named last changes fastest.
Arguments:
- positions: float32 [3, 16, 64, 8, 128], P(None, 'gx', 'gy', 'gz'), may hold values from 0 to 256, as said below
- grain_radii: float32 [16, 64, 8, 128], P('gx', 'gy', 'gz'), may hold values from 0.4 to 0.6
- film_liquid: float32 [16, 64, 8, 128], P('gx', 'gy', 'gz'), may hold values from 0.5 to 2
- pair_live: int32 [4, 16, 4, 864], P('gx', 'gy', 'gz'), may hold values from 0 to 1, as said below
- partner: int32 [4, 16, 4, 864, 128], P('gx', 'gy', 'gz'), may hold values from 0 to 127, as said below
- rupture: int32 [4, 16, 4, 864, 128], P('gx', 'gy', 'gz'), may hold values from 0 to 1
- volume: float32 [4, 16, 4, 864, 128], P('gx', 'gy', 'gz'), may hold values from 0.005 to 0.05
Outputs:
- forces: float32 [3, 16, 64, 8, 128], P(None, 'gx', 'gy', 'gz')
- film_next: float32 [16, 64, 8, 128], P('gx', 'gy', 'gz')
- volume_next: float32 [4, 16, 4, 864, 128], P('gx', 'gy', 'gz')
The draws below stay inside these ranges and needn't reach their ends.
Inputs may be any that keep to these rules, and one draw needn't show every extreme that they name: `pair_live`: slot s of a device is 1 only if its tile pair lies inside the grid; every pair of distinct touching tiles is listed at most once over all devices, by one of its two tiles; the slot of a tile with itself (s % 27 = 13) is always 1. partner[s, m] is never m itself. `positions`: the grains of tile (p, q, r) lie in its box, 8 wide along the first dimension and 4 along the others, the boxes side by side from the root; no two grains are closer than 0.5.
All inputs are finite; a program needn't handle non-finite values.
Results may differ from the reference program's by a relative error of at most 0.0003.
Values sent between devices are 32-bit elements; how exact they have to be, the bound alone decides.
No kernel may reach another device: no remote copies, remote signals or barrier semaphores. Data moves between devices by JAX's collectives and lax.ppermute only.
A program may use at most 64 MiB of HBM per device.

```python
import math
import jax
import jax.numpy as jnp
from jax import lax

GRAINS = 128
BX = 4
BY = 4
BZ = 2
SLOTS = 864
TX = 16
TY = 64
TZ = 8
N_GX = 4
N_GY = 16
N_GZ = 4


shell_offsets = [(along_x, along_y, along_z) for along_x in (-1, 0, 1) for along_y in (-1, 0, 1) for along_z in (-1, 0, 1)]


def site_tables(key):
    scores = jax.random.randint(jax.random.fold_in(key, 41), (TX, TY, TZ, GRAINS), 0, 1048576)
    distinct = scores * GRAINS + jnp.arange(GRAINS, dtype=jnp.int32)
    site_of = jnp.argsort(distinct, axis=-1).astype(jnp.int32)
    grain_at = jnp.argsort(site_of, axis=-1).astype(jnp.int32)
    return (site_of, grain_at)


def draw_positions(key, part):
    site_of = site_tables(key)[0]
    spread = GRAINS // 16
    jitter = jax.random.uniform(key, (3, TX, TY, TZ, GRAINS), jnp.float32, -0.25, 0.25)
    root_x = (jnp.arange(TX, dtype=jnp.int32) * spread).astype(jnp.float32)[:, None, None, None]
    root_y = (jnp.arange(TY, dtype=jnp.int32) * 4).astype(jnp.float32)[None, :, None, None]
    root_z = (jnp.arange(TZ, dtype=jnp.int32) * 4).astype(jnp.float32)[None, None, :, None]
    coord_x = root_x + (site_of // 16).astype(jnp.float32) + 0.5 + jitter[0]
    coord_y = root_y + (site_of // 4 % 4).astype(jnp.float32) + 0.5 + jitter[1]
    coord_z = root_z + (site_of % 4).astype(jnp.float32) + 0.5 + jitter[2]
    return jnp.stack([coord_x, coord_y, coord_z], axis=0)


def bridge_links(key):
    subkeys = jax.random.split(jax.random.fold_in(key, 29), 3)
    site_of, grain_at = site_tables(key)
    layers = GRAINS // 16
    slot_total = 27 * BX * BY * BZ
    shape = (N_GX, N_GY, N_GZ, slot_total, GRAINS)
    full = (N_GX, N_GY, N_GZ, slot_total)
    slot = jnp.arange(slot_total, dtype=jnp.int32)
    tile = slot // 27
    code = slot % 27
    step_x = code // 9 - 1
    step_y = code // 3 % 3 - 1
    step_z = code % 3 - 1
    anchor_x = jnp.broadcast_to((jnp.arange(N_GX, dtype=jnp.int32) * BX)[:, None, None, None] + (tile // (BY * BZ))[None, None, None, :], full)
    anchor_y = jnp.broadcast_to((jnp.arange(N_GY, dtype=jnp.int32) * BY)[None, :, None, None] + (tile // BZ % BY)[None, None, None, :], full)
    anchor_z = jnp.broadcast_to((jnp.arange(N_GZ, dtype=jnp.int32) * BZ)[None, None, :, None] + (tile % BZ)[None, None, None, :], full)
    other_x = jnp.clip(anchor_x + step_x, 0, TX - 1)
    other_y = jnp.clip(anchor_y + step_y, 0, TY - 1)
    other_z = jnp.clip(anchor_z + step_z, 0, TZ - 1)
    site = site_of[anchor_x, anchor_y, anchor_z]
    site_x = site // 16
    site_y = site // 4 % 4
    site_z = site % 4
    heading = jax.random.randint(subkeys[0], shape, 0, 6)
    along = heading // 2
    sign = 2 * (heading % 2) - 1
    target_x = site_x + sign * (along == 0).astype(jnp.int32) - step_x[:, None] * layers
    target_y = site_y + sign * (along == 1).astype(jnp.int32) - step_y[:, None] * 4
    target_z = site_z + sign * (along == 2).astype(jnp.int32) - step_z[:, None] * 4
    inside = (target_x >= 0) & (target_x < layers) & (target_y >= 0) & (target_y < 4) & (target_z >= 0) & (target_z < 4)
    target_site = jnp.where(inside, target_x * 16 + target_y * 4 + target_z, 0).astype(jnp.int32)
    neighbour = jnp.take_along_axis(grain_at[other_x, other_y, other_z], target_site, axis=-1)
    grain = jnp.arange(GRAINS, dtype=jnp.int32)
    stride = jax.random.randint(subkeys[1], shape, 1, GRAINS)
    fallback = (grain + stride) % GRAINS
    partner = jnp.where(inside, neighbour, fallback).astype(jnp.int32)
    chance = jax.random.randint(subkeys[2], shape, 0, 4)
    rupture = jnp.where(inside, (chance == 0).astype(jnp.int32), (chance < 2).astype(jnp.int32)).astype(jnp.int32)
    return (partner, rupture)


def draw_partner(key, part):
    return bridge_links(key)[0]


def draw_rupture(key, part):
    return bridge_links(key)[1]


def draw_pair_live(key, part):
    subkeys = jax.random.split(jax.random.fold_in(key, 11), 3)
    level = jax.random.randint(subkeys[0], (N_GX, N_GY, N_GZ), 1, 7)
    level = jnp.repeat(jnp.repeat(jnp.repeat(level, BX, axis=0), BY, axis=1), BZ, axis=2)
    chance = jax.random.randint(subkeys[1], (13, TX, TY, TZ), 0, 12)
    owner = jax.random.randint(subkeys[2], (13, TX, TY, TZ), 0, 2)
    padded_level = jnp.pad(level, 1)
    inside = jnp.pad(jnp.ones((TX, TY, TZ), jnp.int32), 1)
    table = [jnp.zeros((TX, TY, TZ), jnp.int32) for number in range(27)]
    table[13] = jnp.ones((TX, TY, TZ), jnp.int32)
    upper_half = [offset for offset in shell_offsets if offset > (0, 0, 0)]
    for number, offset in enumerate(upper_half):
        start = (1 + offset[0], 1 + offset[1], 1 + offset[2])
        limit = (1 + offset[0] + TX, 1 + offset[1] + TY, 1 + offset[2] + TZ)
        near_level = lax.slice(padded_level, start, limit)
        near_inside = lax.slice(inside, start, limit)
        listed = (chance[number] < level + near_level) & (near_inside == 1)
        here = (listed & (owner[number] == 0)).astype(jnp.int32)
        there = (listed & (owner[number] == 1)).astype(jnp.int32)
        back_start = (1 - offset[0], 1 - offset[1], 1 - offset[2])
        back_limit = (1 - offset[0] + TX, 1 - offset[1] + TY, 1 - offset[2] + TZ)
        moved = lax.slice(jnp.pad(there, 1), back_start, back_limit)
        table[shell_offsets.index(offset)] = here
        table[shell_offsets.index((-offset[0], -offset[1], -offset[2]))] = moved
    stacked = jnp.stack(table, axis=-1)
    shaped = stacked.reshape(N_GX, BX, N_GY, BY, N_GZ, BZ, 27).transpose(0, 2, 4, 1, 3, 5, 6)
    return shaped.reshape(N_GX, N_GY, N_GZ, 27 * BX * BY * BZ)


def block_scale(stream_key, extent, shards, smallest, largest):
    level = 1.0
    for position, blocks in shards:
        steps = jax.random.uniform(jax.random.fold_in(jax.random.fold_in(stream_key, 6), position), (blocks,), jnp.float32, smallest / len(shards), largest / len(shards))
        level = level * jnp.repeat(jnp.exp(steps), extent[position] // blocks).reshape((-1,) + (1,) * (len(extent) - 1 - position))
    return level


def setup_inputs(seed: int = 0) -> dict:
    key_of = jax.random.split(jax.random.key(seed), 8)
    return {
        "positions": draw_positions(jax.random.fold_in(key_of[7], 71), 0),
        "grain_radii": jnp.clip(0.4 + 0.20000002 * jax.random.uniform(key_of[1], (TX, TY, TZ, GRAINS), jnp.float32) ** block_scale(key_of[1], (TX, TY, TZ, GRAINS), ((0, 4), (1, 16), (2, 4)), -0.2, 0.2), 0.4, 0.6),
        "film_liquid": jnp.clip(0.5 + 1.5 * jax.random.uniform(key_of[2], (TX, TY, TZ, GRAINS), jnp.float32) ** block_scale(key_of[2], (TX, TY, TZ, GRAINS), ((0, 4), (1, 16), (2, 4)), -0.2, 0.2), 0.5, 2.0),
        "pair_live": draw_pair_live(jax.random.fold_in(key_of[7], 71), 0),
        "partner": draw_partner(jax.random.fold_in(key_of[7], 71), 0),
        "rupture": draw_rupture(jax.random.fold_in(key_of[7], 71), 0),
        "volume": jnp.clip(jnp.exp(math.log(0.05) - 2.3025851 * jax.random.uniform(key_of[6], (N_GX, N_GY, N_GZ, SLOTS, GRAINS), jnp.float32) ** block_scale(key_of[6], (N_GX, N_GY, N_GZ, SLOTS, GRAINS), ((0, 4), (1, 16), (2, 4)), -0.2, 0.2)), 0.005, 0.05),
    }


ABSORB = 0.02
shell_offsets = [(along_x, along_y, along_z) for along_x in (-1, 0, 1) for along_y in (-1, 0, 1) for along_z in (-1, 0, 1)]

def evaluate(pieces):
    anchor, others, centre, active, partner, rupture, volume = pieces
    grains = anchor.shape[-1]
    identity = jnp.eye(grains, dtype=jnp.float32)
    diagonal = identity[None] * centre[:, None, None]
    deltas = [anchor[:, component, :, None] - others[:, component, None, :] for component in range(3)]
    squares = deltas[0] * deltas[0] + deltas[1] * deltas[1] + deltas[2] * deltas[2] + diagonal
    distance = jnp.sqrt(squares)
    reach_sum = anchor[:, 3, :, None] + others[:, 3, None, :]
    reduced = anchor[:, 3, :, None] * others[:, 3, None, :] / reach_sum
    intersection = jnp.maximum(reach_sum - distance, 0.0) * (1.0 - diagonal)
    repulse = jnp.sqrt(reduced) * intersection * jnp.sqrt(intersection) / distance * active[:, None, None]
    products = [repulse * member for member in deltas]
    keep_other = (1.0 - centre)[:, None]
    contact_a = jnp.stack([lax.optimization_barrier(jnp.sum(member, axis=2)) for member in products], axis=1)
    contact_b = jnp.stack([-lax.optimization_barrier(jnp.sum(member, axis=1)) * keep_other for member in products], axis=1)
    choose = (partner[:, :, None] == jnp.arange(grains, dtype=jnp.int32)[None, None, :]).astype(jnp.float32)
    matched = jnp.einsum('ncj,nij->nci', others, choose, precision=lax.Precision.HIGHEST)
    gap_vec = anchor[:, :3] - matched[:, :3]
    spacing = jnp.sqrt(lax.optimization_barrier(jnp.sum(gap_vec * gap_vec, axis=1)))
    radius_sum = anchor[:, 3] + matched[:, 3]
    harmonic = 2.0 * anchor[:, 3] * matched[:, 3] / radius_sum
    scaled_gap = jnp.maximum(spacing - radius_sum, 0.0) * jnp.sqrt(harmonic / volume)
    broken = rupture.astype(jnp.float32)
    intact = active[:, None] * (1.0 - broken)
    tension = intact * harmonic / (1.0 + 1.05 * scaled_gap + 2.5 * scaled_gap * scaled_gap) / spacing
    bridge_force = tension[:, None, :] * gap_vec
    released = active[:, None] * broken * volume
    volume_next = intact * (volume + ABSORB * (anchor[:, 4] + matched[:, 4]))
    liquid_anchor = 0.5 * released - ABSORB * intact * anchor[:, 4]
    liquid_other = 0.5 * released - ABSORB * intact * matched[:, 4]
    reaction = jnp.einsum('nci,nij->ncj', jnp.concatenate([bridge_force, liquid_other[:, None]], axis=1), choose, precision=lax.Precision.HIGHEST)
    anchor_side = jnp.concatenate([contact_a - bridge_force, liquid_anchor[:, None]], axis=1)
    other_side = jnp.concatenate([contact_b, jnp.zeros_like(liquid_anchor)[:, None]], axis=1) + reaction
    return (anchor_side, other_side, volume_next)

def tile_order(values):
    extra = values.shape[4:]
    shaped = values.reshape((N_GX, N_GY, N_GZ, BX, BY, BZ, 27) + extra)
    permute = (0, 3, 1, 4, 2, 5, 6) + tuple(range(7, 7 + len(extra)))
    return shaped.transpose(permute).reshape((TX, TY, TZ, 27) + extra)

def reference(positions, grain_radii, film_liquid, pair_live, partner, rupture, volume):
    grain_state = jnp.concatenate([positions, grain_radii[None], film_liquid[None]], axis=0)
    padded = jnp.pad(grain_state, ((0, 0), (1, 1), (1, 1), (1, 1), (0, 0)))
    tile_count = TX * TY * TZ
    groups = tile_count // (BX * BY * BZ)
    active = tile_order(pair_live).astype(jnp.float32)
    partners = tile_order(partner)
    ruptures = tile_order(rupture)
    volumes = tile_order(volume)
    anchor = grain_state.reshape(5, tile_count, GRAINS).transpose(1, 0, 2)
    totals = jnp.zeros((4, TX + 2, TY + 2, TZ + 2, GRAINS), jnp.float32)
    updated = []
    for number, offset in enumerate(shell_offsets):
        start = (0, 1 + offset[0], 1 + offset[1], 1 + offset[2], 0)
        limit = (5, 1 + offset[0] + TX, 1 + offset[1] + TY, 1 + offset[2] + TZ, GRAINS)
        others = lax.slice(padded, start, limit).reshape(5, tile_count, GRAINS).transpose(1, 0, 2)
        centre = jnp.full((tile_count,), 1.0 if number == 13 else 0.0, jnp.float32)
        pieces = (anchor, others, centre, active[:, :, :, number].reshape(tile_count), partners[:, :, :, number].reshape(tile_count, GRAINS), ruptures[:, :, :, number].reshape(tile_count, GRAINS), volumes[:, :, :, number].reshape(tile_count, GRAINS))
        blocked = jax.tree.map(lambda member: member.reshape((groups, tile_count // groups) + member.shape[1:]), pieces)
        anchor_side, other_side, fresh = lax.map(evaluate, blocked)
        anchor_side = anchor_side.reshape(tile_count, 4, GRAINS).transpose(1, 0, 2).reshape(4, TX, TY, TZ, GRAINS)
        other_side = other_side.reshape(tile_count, 4, GRAINS).transpose(1, 0, 2).reshape(4, TX, TY, TZ, GRAINS)
        totals = totals.at[:, 1:TX + 1, 1:TY + 1, 1:TZ + 1].add(anchor_side)
        totals = totals.at[:, 1 + offset[0]:1 + offset[0] + TX, 1 + offset[1]:1 + offset[1] + TY, 1 + offset[2]:1 + offset[2] + TZ].add(other_side)
        updated.append(fresh.reshape(TX, TY, TZ, GRAINS))
    stacked = jnp.stack(updated, axis=3).reshape(N_GX, BX, N_GY, BY, N_GZ, BZ, 27, GRAINS)
    volume_next = stacked.transpose(0, 2, 4, 1, 3, 5, 6, 7).reshape(N_GX, N_GY, N_GZ, 27 * BX * BY * BZ, GRAINS)
    interior = totals[:, 1:TX + 1, 1:TY + 1, 1:TZ + 1]
    return (interior[:3], film_liquid + interior[3], volume_next)
```

```python
import functools

import jax
import jax.numpy as jnp
import numpy as np
from jax import lax
from jax.experimental import pallas as pl
from jax.experimental.pallas import tpu as pltpu
from jax.sharding import PartitionSpec as P

ABSORB = 0.02
BX, BY, BZ = 4, 4, 2
TILES = BX * BY * BZ
SLOTS = 27 * TILES
G = 128
Z_ROWS = 16 * 32
Y_ROWS = 8 * 32 + 8 * 16
X_ROWS = 8 * 32 + 4 * 16 + 8 * 16 + 4 * 8
Z_AT = 0
Y_AT = 2 * Z_ROWS
X_AT = Y_AT + 2 * Y_ROWS
ZERO_AT = X_AT + 2 * X_ROWS
HALO_ROWS = ZERO_AT + 8
BATCH = 32
OFFSETS = [(i, j, k) for i in (-1, 0, 1) for j in (-1, 0, 1) for k in (-1, 0, 1)]


def tile_number(x, y, z):
    return (x * BY + y) * BZ + z


def code(e):
    return 9 * (e[0] + 1) + 3 * (e[1] + 1) + e[2] + 1


def inside(x, y, z):
    return 0 <= x < BX and 0 <= y < BY and 0 <= z < BZ


def halo_block(x, y, z):
    side = lambda v: 0 if v < 0 else 1
    ox, oy, oz = not 0 <= x < BX, not 0 <= y < BY, not 0 <= z < BZ
    if ox:
        base = X_AT + side(x) * X_ROWS
        if oy and oz:
            return base + 448 + (side(y) * 2 + side(z)) * 8, 1
        if oy:
            return base + 256 + (side(y) * 2 + z) * 16, 3
        if oz:
            return base + 320 + (side(z) * 4 + y) * 16, 3
        return base + (y * 2 + z) * 32, 9
    if oy:
        base = Y_AT + side(y) * Y_ROWS
        if oz:
            return base + 256 + (side(z) * 4 + x) * 16, 3
        return base + (x * 2 + z) * 32, 9
    return Z_AT + side(z) * Z_ROWS + (x * 4 + y) * 32, 9


def halo_slot(x, y, z, e):
    base, count = halo_block(x, y, z)
    free = [v + 1 for v, c, n in zip(e, (x, y, z), (BX, BY, BZ)) if 0 <= c < n]
    k = 0
    for v in free:
        k = 3 * k + v
    return base + 5 + k, base + 5 + count + k, base + 5 + 2 * count + k


def pairs():
    for x in range(BX):
        for y in range(BY):
            for z in range(BZ):
                for e in OFFSETS:
                    yield (x, y, z), e, (x + e[0], y + e[1], z + e[2])


def pad(rows, multiple, dummy):
    rows = list(rows)
    while len(rows) % multiple:
        rows.append(dummy)
    return rows


def bridge_tables():
    inner, outward, inward = [], [], []
    for t, e, b in pairs():
        own = 8 * tile_number(*t)
        s = 27 * tile_number(*t) + code(e)
        if inside(*b):
            inner.append((own, 8 * tile_number(*b), s, s, s))
        else:
            back = tuple(-v for v in e)
            outward.append((own, halo_block(*b)[0], s, s, s))
            inward.append((halo_block(*b)[0], own) + halo_slot(*b, back))
    return inner, outward, inward


def contact_class(e):
    kinds = sum(abs(v) for v in e)
    if kinds == 0:
        return 3
    if kinds > 1:
        return 0
    return 1 if e[0] else 2


CHUNKS = (1, 2, 4, 16)
UNROLL = (16, 8, 4, 2)


def contact_tables(halo):
    out = [[], [], [], []]
    for t, e, b in pairs():
        own = 8 * tile_number(*t)
        s = 27 * tile_number(*t) + code(e)
        back = tuple(-v for v in e)
        kind = contact_class(e)
        if inside(*b):
            s2 = 27 * tile_number(*b) + code(back)
            if not halo:
                out[kind].append((own, 8 * tile_number(*b), s, s2, s2))
        elif halo:
            _, ret, rel = halo_slot(*b, back)
            out[kind].append((own, halo_block(*b)[0], s, ret, rel))
    return out


def flat(rows):
    return np.asarray(rows, np.int32).reshape(-1)


def row(ref, at):
    return ref[pl.ds(at, 1), :]


def block(ref, at):
    return ref[pl.ds(pl.multiple_of(at, 8), 8), :]


def run_bridges(count, tab, a_ref, b_ref, p_ref, q_ref, l_ref, scr, acc_a, acc_b, next_ref):
    m_ref, a_scr, q_scr, l_scr, f_ref, g_ref = scr

    def body(i, carry):
        at = []
        for j in range(BATCH):
            o = (i * BATCH + j) * 5
            at.append([tab[o + k] for k in range(5)])
        partner = []
        for j in range(BATCH):
            a, b, p, q, l = at[j]
            idx = row(p_ref, p).astype(jnp.int32)
            m_ref[8 * j : 8 * j + 8, :] = jnp.take_along_axis(
                block(b_ref, b), jnp.broadcast_to(idx, (8, G)), axis=1
            )
            a_scr[8 * j : 8 * j + 8, :] = block(a_ref, a)
            q_scr[j : j + 1, :] = row(q_ref, q)
            l_scr[j : j + 1, :] = row(l_ref, l)
        for g in range(BATCH // 8):
            near = [m_ref[pl.ds(64 * g + c, 8, stride=8), :] for c in range(5)]
            own = [a_scr[pl.ds(64 * g + c, 8, stride=8), :] for c in range(5)]
            held = q_scr[8 * g : 8 * g + 8, :]
            half = 0.5 * l_scr[8 * g : 8 * g + 8, :]
            gap = [own[c] - near[c] for c in range(3)]
            squares = gap[0] * gap[0] + gap[1] * gap[1] + gap[2] * gap[2]
            inverse = lax.rsqrt(squares)
            spacing = squares * inverse
            radius_sum = own[3] + near[3]
            harmonic = 2.0 * own[3] * near[3] / radius_sum
            scaled = (
                jnp.maximum(spacing - radius_sum, 0.0) * harmonic * lax.rsqrt(harmonic * held)
            )
            intact = held > 0.0
            tension = harmonic * inverse / (1.0 + 1.05 * scaled + 2.5 * scaled * scaled)
            tension = jnp.where(intact, tension, 0.0)
            absorb = jnp.where(intact, ABSORB, 0.0)
            force = [tension * gap[c] for c in range(3)]
            if acc_b is not None:
                for c, value in enumerate(force + [half - absorb * near[4]]):
                    high = value.astype(jnp.bfloat16).astype(jnp.float32)
                    f_ref[pl.ds(64 * g + c, 8, stride=8), :] = high
                    f_ref[pl.ds(64 * g + 4 + c, 8, stride=8), :] = value - high
            if acc_a is not None:
                for c in range(3):
                    g_ref[pl.ds(64 * g + c, 8, stride=8), :] = -force[c]
                g_ref[pl.ds(64 * g + 3, 8, stride=8), :] = half - absorb * own[4]
                g_ref[pl.ds(64 * g + 4, 8, stride=8), :] = jnp.where(
                    intact, held + ABSORB * (own[4] + near[4]), 0.0
                )
        if acc_a is not None:
            for j in range(BATCH):
                a, b, p, q, l = at[j]
                here = pl.ds(pl.multiple_of(a, 8), 8)
                acc_a[here, :] = acc_a[here, :] + g_ref[8 * j : 8 * j + 8, :]
                next_ref[pl.ds(p, 1), :] = g_ref[8 * j + 4 : 8 * j + 5, :]
        if acc_b is not None:
            sub = lax.broadcasted_iota(jnp.int32, (G, G), 0)
            for j in range(BATCH):
                a, b, p, q, l = at[j]
                idx = row(p_ref, p).astype(jnp.int32)
                choose = (sub == idx).astype(jnp.bfloat16)
                landed = lax.dot_general(
                    f_ref[8 * j : 8 * j + 8, :].astype(jnp.bfloat16),
                    choose,
                    (((1,), (1,)), ((), ())),
                    preferred_element_type=jnp.float32,
                )
                here = pl.ds(pl.multiple_of(b, 8), 8)
                acc_b[here, :] = acc_b[here, :] + landed
        return carry

    lax.fori_loop(0, count // BATCH, body, 0)


def chunk_force(key, base, other, target):
    sub = lax.broadcasted_iota(jnp.int32, (8, G), 0).astype(jnp.float32) + base
    chosen = key == sub
    rows = [
        jnp.sum(jnp.where(chosen, other[c], 0.0), axis=1, keepdims=True) for c in range(4)
    ]
    radius = jnp.where(rows[3] > 0.0, rows[3], -1000.0)
    delta = [target[c] - rows[c] for c in range(3)]
    squares = delta[0] * delta[0] + delta[1] * delta[1] + delta[2] * delta[2]
    squares = jnp.maximum(squares, 1e-6)
    inverse = lax.rsqrt(squares)
    reach = target[3] + radius
    overlap = jnp.maximum(reach - squares * inverse, 0.0)
    weight = target[3] * radius * overlap
    push = overlap * inverse * weight * lax.rsqrt(jnp.maximum(weight * reach, 1e-30))
    return [push * delta[c] for c in range(3)]


def run_contacts(sizes, tab, t_ref, n_ref, q_ref, l_ref, nq_ref, nl_ref, low, high, mark, keys, acc):
    total = sum(sizes)
    wide = lax.broadcasted_iota(jnp.int32, (8, G), 0)

    def near(i, carry):
        for u in range(16):
            j = i * 16 + u
            t, n, s, nq, nl = [tab[j * 5 + k] for k in range(5)]
            live = row(q_ref, s) + row(l_ref, s) + row(nq_ref, nq) + row(nl_ref, nl) > 0.0
            value = block(n_ref, n)
            top = block(high, t)
            gap = jnp.maximum(jnp.maximum(block(low, t) - value, value - top), 0.0)
            gap = jnp.where(wide < 3, gap * gap, 0.0)
            distance = jnp.sum(gap, axis=0, keepdims=True)
            limit = value[3:4, :] + top[3:4, :] + 0.001
            mark[pl.ds(j, 1), :] = jnp.where(
                live & (distance <= limit * limit), 1.0, 0.0
            )
        return carry

    lax.fori_loop(0, total // 16, near, 0)
    lane = lax.broadcasted_iota(jnp.int32, (G, G), 1)
    sub = lax.broadcasted_iota(jnp.int32, (G, G), 0)
    upper = (sub <= lane).astype(jnp.bfloat16)
    start = 0
    crowded = []
    for kind, size in enumerate(sizes):
        if not size:
            continue
        if kind == 3:
            keys[start : start + size, :] = lax.broadcasted_iota(
                jnp.int32, (size, G), 1
            ).astype(jnp.float32)
        else:
            held = mark[start : start + size, :]
            rank = jnp.dot(
                held.astype(jnp.bfloat16), upper, preferred_element_type=jnp.float32
            )
            keys[start : start + size, :] = jnp.where(held > 0.0, rank - 1.0, -1.0)
            crowded.append((kind, start, size, jnp.max(rank) > 8.0 * CHUNKS[kind]))
        start += size

    def job(j, chunk_list):
        t, n = tab[j * 5], tab[j * 5 + 1]
        target = block(t_ref, t)
        other = block(n_ref, n)
        target = [target[c : c + 1, :] for c in range(4)]
        other = [other[c : c + 1, :] for c in range(4)]
        key = row(keys, j)
        force = None
        for base in chunk_list:
            part = chunk_force(key, base, other, target)
            force = part if force is None else [x + y for x, y in zip(force, part)]
        for c in range(3):
            here = pl.ds(pl.multiple_of(t * 3 + 8 * c, 8), 8)
            acc[here, :] = acc[here, :] + force[c]

    start = 0
    for kind, size in enumerate(sizes):
        if not size:
            continue
        unroll = UNROLL[kind]

        def body(i, carry, start=start, kind=kind, unroll=unroll):
            for u in range(unroll):
                job(start + i * unroll + u, [8.0 * c for c in range(CHUNKS[kind])])
            return carry

        lax.fori_loop(0, size // unroll, body, 0)
        start += size

    for kind, start, size, over in crowded:

        @pl.when(over)
        def _(kind=kind, start=start, size=size):
            def rest(j, carry):
                def one(c, inner):
                    job(start + j, [8.0 * c.astype(jnp.float32)])
                    return inner

                return lax.fori_loop(CHUNKS[kind], 16, one, carry)

            lax.fori_loop(0, size, rest, 0)


def bounds(st_ref, low, high):
    for t in range(TILES):
        value = st_ref[8 * t : 8 * t + 8, :]
        low[8 * t : 8 * t + 8, :] = jnp.broadcast_to(
            jnp.min(value, axis=1, keepdims=True), (8, G)
        )
        high[8 * t : 8 * t + 8, :] = jnp.broadcast_to(
            jnp.max(value, axis=1, keepdims=True), (8, G)
        )


def settle(acc):
    rows = []
    for t in range(TILES):
        for c in range(3):
            at = 24 * t + 8 * c
            rows.append(jnp.sum(acc[at : at + 8, :], axis=0, keepdims=True))
    return rows


def inner_kernel(sizes, count, tab_b, tab_c, st, part, ret, rel, total, fresh, *scr):
    *bridge, acc_a, acc_b, low, high, mark, keys, acc = scr
    acc_a[...] = jnp.zeros_like(acc_a)
    acc_b[...] = jnp.zeros_like(acc_b)
    acc[...] = jnp.zeros_like(acc)
    bounds(st, low, high)
    run_contacts(sizes, tab_c, st, st, ret, rel, ret, rel, low, high, mark, keys, acc)
    run_bridges(count, tab_b, st, st, part, ret, rel, bridge, acc_a, acc_b, fresh)
    rows = settle(acc)
    for t in range(TILES):
        at = 8 * t
        held = acc_a[at : at + 4, :] + acc_b[at : at + 4, :] + acc_b[at + 4 : at + 8, :]
        total[at : at + 4, :] = held
        for c in range(3):
            total[at + c : at + c + 1, :] = held[c : c + 1, :] + rows[3 * t + c]


def halo_kernel(
    sizes, n_out, n_in, tab_o, tab_i, tab_c, st, part, ret, rel, held, before,
    za, zb, ya, yb, xa, xb, forces, film, fresh, *scr
):
    *bridge, acc_a, acc_b, low, high, mark, keys, acc, halo, sems = scr
    copies = []
    for k, (pair, axis, at, rows) in enumerate(
        (((za, zb), "gz", Z_AT, Z_ROWS), ((ya, yb), "gy", Y_AT, Y_ROWS), ((xa, xb), "gx", X_AT, X_ROWS))
    ):
        odd = lax.axis_index(axis) % 2
        for w, src in enumerate(pair):
            side = (1 - odd) if w == 0 else odd
            copy = pltpu.make_async_copy(
                src, halo.at[pl.ds(at + side * rows, rows), :], sems.at[2 * k + w]
            )
            copy.start()
            copies.append(copy)
    keep = pltpu.make_async_copy(before, fresh, sems.at[6])
    keep.start()
    acc_a[...] = held[...]
    acc_b[...] = jnp.zeros_like(acc_b)
    acc[...] = jnp.zeros_like(acc)
    halo[ZERO_AT : ZERO_AT + 8, :] = jnp.zeros((8, G), jnp.float32)
    bounds(st, low, high)
    for copy in copies:
        copy.wait()
    keep.wait()
    run_contacts(sizes, tab_c, st, halo, ret, rel, halo, halo, low, high, mark, keys, acc)
    run_bridges(n_out, tab_o, st, halo, part, ret, rel, bridge, acc_a, None, fresh)
    run_bridges(n_in, tab_i, halo, st, halo, halo, halo, bridge, None, acc_b, None)
    rows = settle(acc)
    for t in range(TILES):
        at = 8 * t
        value = acc_a[at : at + 4, :] + acc_b[at : at + 4, :] + acc_b[at + 4 : at + 8, :]
        for c in range(3):
            forces[c, t : t + 1, :] = value[c : c + 1, :] + rows[3 * t + c]
        film[t : t + 1, :] = value[3:4, :] + st[at + 4 : at + 5, :]


def send_sides(axis):
    odd = lax.axis_index(axis) % 2
    return 1 - odd, odd


def own_slots(refs, at):
    return [ref[pl.ds(at, 9), :].astype(jnp.float32) for ref in refs]


def pack_z_kernel(pos, rad, film, part, ret, rel, st, out_a, out_b):
    for g in range(TILES // 8):
        members = [pos[c, 8 * g : 8 * g + 8, :] for c in range(3)]
        members += [rad[8 * g : 8 * g + 8, :], film[8 * g : 8 * g + 8, :]]
        for c, value in enumerate(members):
            st[pl.ds(64 * g + c, 8, stride=8), :] = value
        for c in range(5, 8):
            st[pl.ds(64 * g + c, 8, stride=8), :] = jnp.zeros((8, G), jnp.float32)
    for out, side in zip((out_a, out_b), send_sides("gz")):
        for xy in range(16):
            t = 2 * xy + side
            at = 32 * xy
            out[at : at + 5, :] = st[pl.ds(8 * t, 5), :]
            for k, ref in enumerate((part, ret, rel)):
                rows = ref[pl.ds(27 * t + 2 * side, 9, stride=3), :]
                out[at + 5 + 9 * k : at + 14 + 9 * k, :] = rows.astype(jnp.float32)


def load_sides(pair, axis, buf, rows, sems, first):
    odd = lax.axis_index(axis) % 2
    copies = []
    for w, src in enumerate(pair):
        side = (1 - odd) if w == 0 else odd
        copy = pltpu.make_async_copy(src, buf.at[pl.ds(side * rows, rows), :], sems.at[first + w])
        copy.start()
        copies.append(copy)
    return copies


def pack_y_kernel(st, part, ret, rel, za, zb, out_a, out_b, zbuf, sems):
    for copy in load_sides((za, zb), "gz", zbuf, Z_ROWS, sems, 0):
        copy.wait()
    for out, side in zip((out_a, out_b), send_sides("gy")):
        for x in range(4):
            for z in range(2):
                t = tile_number(x, 3 * side, z)
                at = 32 * (2 * x + z)
                out[at : at + 5, :] = st[pl.ds(8 * t, 5), :]
                for k, ref in enumerate((part, ret, rel)):
                    for i in range(3):
                        here = at + 5 + 9 * k + 3 * i
                        rows = ref[pl.ds(27 * t + 9 * i + 6 * side, 3), :]
                        out[here : here + 3, :] = rows.astype(jnp.float32)
        for sz in range(2):
            for x in range(4):
                at = 256 + 16 * (4 * sz + x)
                src = sz * Z_ROWS + (x * 4 + 3 * side) * 32
                out[at : at + 5, :] = zbuf[pl.ds(src, 5), :]
                for k in range(3):
                    out[at + 5 + 3 * k : at + 8 + 3 * k, :] = zbuf[
                        pl.ds(src + 5 + 9 * k + 2 * side, 3, stride=3), :
                    ]
                out[at + 14 : at + 16, :] = jnp.zeros((2, G), jnp.float32)


def pack_x_kernel(st, part, ret, rel, za, zb, ya, yb, out_a, out_b, zbuf, ybuf, sems):
    copies = load_sides((za, zb), "gz", zbuf, Z_ROWS, sems, 0)
    copies += load_sides((ya, yb), "gy", ybuf, Y_ROWS, sems, 2)
    for copy in copies:
        copy.wait()
    for out, side in zip((out_a, out_b), send_sides("gx")):
        for y in range(4):
            for z in range(2):
                t = tile_number(3 * side, y, z)
                at = 32 * (2 * y + z)
                out[at : at + 5, :] = st[pl.ds(8 * t, 5), :]
                for k, ref in enumerate((part, ret, rel)):
                    rows = ref[pl.ds(27 * t + 18 * side, 9), :]
                    out[at + 5 + 9 * k : at + 14 + 9 * k, :] = rows.astype(jnp.float32)
        for sy in range(2):
            for z in range(2):
                at = 256 + 16 * (2 * sy + z)
                src = sy * Y_ROWS + (2 * 3 * side + z) * 32
                out[at : at + 5, :] = ybuf[pl.ds(src, 5), :]
                for k in range(3):
                    out[at + 5 + 3 * k : at + 8 + 3 * k, :] = ybuf[
                        pl.ds(src + 5 + 9 * k + 6 * side, 3), :
                    ]
                out[at + 14 : at + 16, :] = jnp.zeros((2, G), jnp.float32)
        for sz in range(2):
            for y in range(4):
                at = 320 + 16 * (4 * sz + y)
                src = sz * Z_ROWS + (4 * 3 * side + y) * 32
                out[at : at + 5, :] = zbuf[pl.ds(src, 5), :]
                for k in range(3):
                    out[at + 5 + 3 * k : at + 8 + 3 * k, :] = zbuf[
                        pl.ds(src + 5 + 9 * k + 6 * side, 3), :
                    ]
                out[at + 14 : at + 16, :] = jnp.zeros((2, G), jnp.float32)
        for sy in range(2):
            for sz in range(2):
                at = 448 + 8 * (2 * sy + sz)
                src = sy * Y_ROWS + 256 + 16 * (4 * sz + 3 * side)
                out[at : at + 5, :] = ybuf[pl.ds(src, 5), :]
                for k in range(3):
                    out[at + 5 + k : at + 6 + k, :] = ybuf[
                        pl.ds(src + 5 + 3 * k + 2 * side, 1), :
                    ]


VM = pl.BlockSpec(memory_space=pltpu.VMEM)
SM = pl.BlockSpec(memory_space=pltpu.SMEM)
AN = pl.BlockSpec(memory_space=pl.ANY)
PARAMS = pltpu.CompilerParams(vmem_limit_bytes=48 * 1024 * 1024)


def rows_of(n):
    return jax.ShapeDtypeStruct((n, G), jnp.float32)


def swap(pair, axis):
    count = lax.axis_size(axis)
    first, second = pair
    near = [(i, i ^ 1) for i in range(count) if i ^ 1 < count]
    far = [(i, ((i + 1) ^ 1) - 1) for i in range(1, count) if ((i + 1) ^ 1) - 1 < count]
    return lax.ppermute(first, axis, near), lax.ppermute(second, axis, far)


def bridge_scratch():
    return [
        pltpu.VMEM((8 * BATCH, G), jnp.float32),
        pltpu.VMEM((8 * BATCH, G), jnp.float32),
        pltpu.VMEM((BATCH, G), jnp.float32),
        pltpu.VMEM((BATCH, G), jnp.float32),
        pltpu.VMEM((8 * BATCH, G), jnp.float32),
        pltpu.VMEM((8 * BATCH, G), jnp.float32),
    ]


def work_scratch(jobs):
    return bridge_scratch() + [
        pltpu.VMEM((8 * TILES, G), jnp.float32),
        pltpu.VMEM((8 * TILES, G), jnp.float32),
        pltpu.VMEM((8 * TILES, G), jnp.float32),
        pltpu.VMEM((8 * TILES, G), jnp.float32),
        pltpu.VMEM((jobs, G), jnp.float32),
        pltpu.VMEM((jobs, G), jnp.float32),
        pltpu.VMEM((24 * TILES, G), jnp.float32),
    ]


def shards(positions, grain_radii, film_liquid, pair_live, partner, rupture, volume):
    pos = positions.reshape(3, TILES, G)
    rad = grain_radii.reshape(TILES, G)
    film = film_liquid.reshape(TILES, G)
    part = partner.reshape(SLOTS, G)
    vol = volume.reshape(SLOTS, G)
    live = pair_live.reshape(SLOTS, 1) > 0
    broken = rupture.reshape(SLOTS, G) > 0
    ret = jnp.where(live & ~broken, vol, 0.0)
    rel = jnp.where(live & broken, vol, 0.0)

    st, za, zb = pl.pallas_call(
        pack_z_kernel,
        out_shape=(rows_of(8 * TILES), rows_of(Z_ROWS), rows_of(Z_ROWS)),
        in_specs=[VM] * 6,
        out_specs=(VM,) * 3,
        compiler_params=PARAMS,
        name="pack_z",
    )(pos, rad, film, part, ret, rel)
    za, zb = swap((za, zb), "gz")
    ya, yb = pl.pallas_call(
        pack_y_kernel,
        out_shape=(rows_of(Y_ROWS),) * 2,
        in_specs=[VM] * 4 + [AN] * 2,
        out_specs=(VM,) * 2,
        scratch_shapes=[pltpu.VMEM((2 * Z_ROWS, G), jnp.float32), pltpu.SemaphoreType.DMA((2,))],
        compiler_params=PARAMS,
        name="pack_y",
    )(st, part, ret, rel, za, zb)
    ya, yb = swap((ya, yb), "gy")
    xa, xb = pl.pallas_call(
        pack_x_kernel,
        out_shape=(rows_of(X_ROWS),) * 2,
        in_specs=[VM] * 4 + [AN] * 4,
        out_specs=(VM,) * 2,
        scratch_shapes=[
            pltpu.VMEM((2 * Z_ROWS, G), jnp.float32),
            pltpu.VMEM((2 * Y_ROWS, G), jnp.float32),
            pltpu.SemaphoreType.DMA((4,)),
        ],
        compiler_params=PARAMS,
        name="pack_x",
    )(st, part, ret, rel, za, zb, ya, yb)
    xa, xb = swap((xa, xb), "gx")

    inner, outward, inward = bridge_tables()
    near = contact_tables(False)
    zero = SLOTS
    near = [pad(rows, UNROLL[k] if k else 16, (0, 0, zero, zero, zero)) for k, rows in enumerate(near)]
    inner = pad(inner, BATCH, (0, 0, zero, zero, zero))
    sizes = tuple(len(rows) for rows in near)
    extra = jnp.zeros((8, G), jnp.float32)
    part_pad = jnp.concatenate([part, jnp.zeros((8, G), jnp.int32)], axis=0)
    ret_pad = jnp.concatenate([ret, extra], axis=0)
    rel_pad = jnp.concatenate([rel, extra], axis=0)
    tab_c = flat(sum(near, []))
    tab_b = flat(inner)
    held, fresh = pl.pallas_call(
        functools.partial(inner_kernel, sizes, len(inner)),
        out_shape=(rows_of(8 * TILES), rows_of(SLOTS + 8)),
        in_specs=[SM] * 2 + [VM] * 4,
        out_specs=(VM,) * 2,
        scratch_shapes=work_scratch(sum(sizes)),
        compiler_params=PARAMS,
        name="inner",
    )(tab_b, tab_c, st, part_pad, ret_pad, rel_pad)

    far = contact_tables(True)
    far = [pad(rows, UNROLL[k] if k else 16, (0, 0, zero, ZERO_AT, ZERO_AT)) for k, rows in enumerate(far)]
    sizes = tuple(len(rows) for rows in far)
    outward = pad(outward, BATCH, (0, 0, zero, zero, zero))
    inward = pad(inward, BATCH, (0, 0, ZERO_AT, ZERO_AT, ZERO_AT))
    forces, film_next, fresh = pl.pallas_call(
        functools.partial(halo_kernel, sizes, len(outward), len(inward)),
        out_shape=(
            jax.ShapeDtypeStruct((3, TILES, G), jnp.float32),
            rows_of(TILES),
            rows_of(SLOTS + 8),
        ),
        in_specs=[SM] * 3 + [VM] * 5 + [AN] * 7,
        out_specs=(VM,) * 3,
        scratch_shapes=work_scratch(sum(sizes))
        + [pltpu.VMEM((HALO_ROWS, G), jnp.float32), pltpu.SemaphoreType.DMA((7,))],
        compiler_params=PARAMS,
        name="halo",
    )(
        flat(outward), flat(inward), flat(sum(far, [])),
        st, part_pad, ret_pad, rel_pad, held, fresh, za, zb, ya, yb, xa, xb,
    )
    return (
        forces.reshape(positions.shape),
        film_next.reshape(film_liquid.shape),
        fresh[:SLOTS].reshape(volume.shape),
    )


def solution(mesh):
    return jax.shard_map(
        shards,
        mesh=mesh,
        in_specs=(
            P(None, "gx", "gy", "gz", None),
            P("gx", "gy", "gz", None),
            P("gx", "gy", "gz", None),
            P("gx", "gy", "gz", None),
            P("gx", "gy", "gz", None, None),
            P("gx", "gy", "gz", None, None),
            P("gx", "gy", "gz", None, None),
        ),
        out_specs=(
            P(None, "gx", "gy", "gz", None),
            P("gx", "gy", "gz", None),
            P("gx", "gy", "gz", None, None),
        ),
        check_vma=False,
    )
```

```python
import functools

import jax
import jax.numpy as jnp
import numpy as np
from jax import lax
from jax.experimental import pallas as pl
from jax.experimental.pallas import tpu as pltpu
from jax.sharding import PartitionSpec as P

ABSORB = 0.02
BX, BY, BZ = 4, 4, 2
TILES = BX * BY * BZ
SLOTS = 27 * TILES
G = 128
Z_ROWS = 16 * 32
Y_ROWS = 8 * 32 + 8 * 16
X_ROWS = 8 * 32 + 4 * 16 + 8 * 16 + 4 * 8
Z_AT = 0
Y_AT = 2 * Z_ROWS
X_AT = Y_AT + 2 * Y_ROWS
ZERO_AT = X_AT + 2 * X_ROWS
HALO_ROWS = ZERO_AT + 8
BATCH = 32
OFFSETS = [(i, j, k) for i in (-1, 0, 1) for j in (-1, 0, 1) for k in (-1, 0, 1)]


def tile_number(x, y, z):
    return (x * BY + y) * BZ + z


def code(e):
    return 9 * (e[0] + 1) + 3 * (e[1] + 1) + e[2] + 1


def inside(x, y, z):
    return 0 <= x < BX and 0 <= y < BY and 0 <= z < BZ


def halo_block(x, y, z):
    side = lambda v: 0 if v < 0 else 1
    ox, oy, oz = not 0 <= x < BX, not 0 <= y < BY, not 0 <= z < BZ
    if ox:
        base = X_AT + side(x) * X_ROWS
        if oy and oz:
            return base + 448 + (side(y) * 2 + side(z)) * 8, 1
        if oy:
            return base + 256 + (side(y) * 2 + z) * 16, 3
        if oz:
            return base + 320 + (side(z) * 4 + y) * 16, 3
        return base + (y * 2 + z) * 32, 9
    if oy:
        base = Y_AT + side(y) * Y_ROWS
        if oz:
            return base + 256 + (side(z) * 4 + x) * 16, 3
        return base + (x * 2 + z) * 32, 9
    return Z_AT + side(z) * Z_ROWS + (x * 4 + y) * 32, 9


def halo_slot(x, y, z, e):
    base, count = halo_block(x, y, z)
    free = [v + 1 for v, c, n in zip(e, (x, y, z), (BX, BY, BZ)) if 0 <= c < n]
    k = 0
    for v in free:
        k = 3 * k + v
    return base + 5 + k, base + 5 + count + k, base + 5 + 2 * count + k


def pairs():
    for x in range(BX):
        for y in range(BY):
            for z in range(BZ):
                for e in OFFSETS:
                    yield (x, y, z), e, (x + e[0], y + e[1], z + e[2])


def pad(rows, multiple, dummy):
    rows = list(rows)
    while len(rows) % multiple:
        rows.append(dummy)
    return rows


def bridge_tables():
    inner, outward, inward = [], [], [[], [], [], []]
    for t, e, b in pairs():
        own = 8 * tile_number(*t)
        s = 27 * tile_number(*t) + code(e)
        if inside(*b):
            inner.append((own, 8 * tile_number(*b), s, s, s))
        else:
            back = tuple(-v for v in e)
            outward.append((own, halo_block(*b)[0], s, s, s))
            inward[contact_class(e)].append((halo_block(*b)[0], own) + halo_slot(*b, back))
    return inner, outward, sum(inward, [])


def contact_class(e):
    kinds = sum(abs(v) for v in e)
    if kinds == 0:
        return 3
    if kinds > 1:
        return 0
    return 1 if e[0] else 2


CHUNKS = (1, 2, 4, 16)
UNROLL = (80, 16, 16, 4)


def contact_tables(halo):
    out = [[], [], [], []]
    for t, e, b in pairs():
        own = 8 * tile_number(*t)
        s = 27 * tile_number(*t) + code(e)
        back = tuple(-v for v in e)
        kind = contact_class(e)
        if inside(*b):
            s2 = 27 * tile_number(*b) + code(back)
            if not halo:
                out[kind].append((own, 8 * tile_number(*b), s, s2, s2))
        elif halo:
            _, ret, rel = halo_slot(*b, back)
            out[kind].append((own, halo_block(*b)[0], s, ret, rel))
    return out


def flat(rows):
    return np.asarray(rows, np.int32).reshape(-1)


def row(ref, at):
    return ref[pl.ds(at, 1), :]


def block(ref, at):
    return ref[pl.ds(pl.multiple_of(at, 8), 8), :]


def compact(count, listed, jobs):
    def body(i, n):
        for u in range(16):
            j = i * 16 + u
            jobs[n] = j
            n = n + listed(j)
        return n

    n = lax.fori_loop(0, count // 16, body, 0)
    for u in range(BATCH):
        jobs[n + u] = count
    return (n + BATCH - 1) // BATCH


def run_bridges(batches, jobs, tab, a_ref, b_ref, p_ref, q_ref, l_ref, scr, acc_a, acc_b, next_ref):
    m_ref, a_scr, q_scr, l_scr, f_ref, g_ref = scr

    def body(i, carry):
        at = []
        for j in range(BATCH):
            o = jobs[i * BATCH + j] * 5
            at.append([tab[o + k] for k in range(5)])
        partner = []
        for j in range(BATCH):
            a, b, p, q, l = at[j]
            idx = row(p_ref, p).astype(jnp.int32)
            m_ref[8 * j : 8 * j + 8, :] = jnp.take_along_axis(
                block(b_ref, b), jnp.broadcast_to(idx, (8, G)), axis=1
            )
            a_scr[8 * j : 8 * j + 8, :] = block(a_ref, a)
            q_scr[j : j + 1, :] = row(q_ref, q)
            l_scr[j : j + 1, :] = row(l_ref, l)
        for g in range(BATCH // 8):
            near = [m_ref[pl.ds(64 * g + c, 8, stride=8), :] for c in range(5)]
            own = [a_scr[pl.ds(64 * g + c, 8, stride=8), :] for c in range(5)]
            held = q_scr[8 * g : 8 * g + 8, :]
            half = 0.5 * l_scr[8 * g : 8 * g + 8, :]
            gap = [own[c] - near[c] for c in range(3)]
            squares = gap[0] * gap[0] + gap[1] * gap[1] + gap[2] * gap[2]
            inverse = lax.rsqrt(squares)
            spacing = squares * inverse
            radius_sum = own[3] + near[3]
            harmonic = 2.0 * own[3] * near[3] / radius_sum
            scaled = (
                jnp.maximum(spacing - radius_sum, 0.0) * harmonic * lax.rsqrt(harmonic * held)
            )
            intact = held > 0.0
            tension = harmonic * inverse / (1.0 + 1.05 * scaled + 2.5 * scaled * scaled)
            tension = jnp.where(intact, tension, 0.0)
            absorb = jnp.where(intact, ABSORB, 0.0)
            force = [tension * gap[c] for c in range(3)]
            if acc_b is not None:
                for c, value in enumerate(force + [half - absorb * near[4]]):
                    high = value.astype(jnp.bfloat16).astype(jnp.float32)
                    f_ref[pl.ds(64 * g + c, 8, stride=8), :] = high
                    f_ref[pl.ds(64 * g + 4 + c, 8, stride=8), :] = value - high
            if acc_a is not None:
                for c in range(3):
                    g_ref[pl.ds(64 * g + c, 8, stride=8), :] = -force[c]
                g_ref[pl.ds(64 * g + 3, 8, stride=8), :] = half - absorb * own[4]
                g_ref[pl.ds(64 * g + 4, 8, stride=8), :] = jnp.where(
                    intact, held + ABSORB * (own[4] + near[4]), 0.0
                )
        if acc_a is not None:
            for j in range(BATCH):
                a, b, p, q, l = at[j]
                here = pl.ds(pl.multiple_of(a, 8), 8)
                acc_a[here, :] = acc_a[here, :] + g_ref[8 * j : 8 * j + 8, :]
                next_ref[pl.ds(p, 1), :] = g_ref[8 * j + 4 : 8 * j + 5, :]
        if acc_b is not None:
            sub = lax.broadcasted_iota(jnp.int32, (G, G), 0)
            for j in range(BATCH):
                a, b, p, q, l = at[j]
                idx = row(p_ref, p).astype(jnp.int32)
                choose = (sub == idx).astype(jnp.bfloat16)
                landed = lax.dot_general(
                    f_ref[8 * j : 8 * j + 8, :].astype(jnp.bfloat16),
                    choose,
                    (((1,), (1,)), ((), ())),
                    preferred_element_type=jnp.float32,
                )
                here = pl.ds(pl.multiple_of(b, 8), 8)
                acc_b[here, :] = acc_b[here, :] + landed
        return carry

    lax.fori_loop(0, batches, body, 0)


def chunk_force(key, base, other, target):
    sub = lax.broadcasted_iota(jnp.int32, (8, G), 0).astype(jnp.float32) + base
    chosen = key == sub
    rows = [
        jnp.sum(jnp.where(chosen, other[c], 0.0), axis=1, keepdims=True) for c in range(4)
    ]
    radius = jnp.where(rows[3] > 0.0, rows[3], -1000.0)
    delta = [target[c] - rows[c] for c in range(3)]
    squares = delta[0] * delta[0] + delta[1] * delta[1] + delta[2] * delta[2]
    squares = jnp.maximum(squares, 1e-6)
    inverse = lax.rsqrt(squares)
    reach = target[3] + radius
    overlap = jnp.maximum(reach - squares * inverse, 0.0)
    weight = target[3] * radius * overlap
    push = overlap * inverse * weight * lax.rsqrt(jnp.maximum(weight * reach, 1e-30))
    return [push * delta[c] for c in range(3)]


def run_contacts(sizes, tab, t_ref, n_ref, q_ref, l_ref, nq_ref, nl_ref, low, high, mark, keys, seen, acc):
    total = sum(sizes)
    step = max(k for k in range(1, 81) if total % k == 0)
    wide = lax.broadcasted_iota(jnp.int32, (8, G), 0)

    def near(i, carry):
        for u in range(step):
            j = i * step + u
            t, n, s, nq, nl = [tab[j * 5 + k] for k in range(5)]
            theirs = row(nq_ref, nq) + row(nl_ref, nl)
            if seen is not None:
                seen[pl.ds(j, 1), :] = theirs
            live = row(q_ref, s) + row(l_ref, s) + theirs > 0.0
            value = block(n_ref, n)
            top = block(high, t)
            gap = jnp.maximum(jnp.maximum(block(low, t) - value, value - top), 0.0)
            gap = jnp.where(wide < 3, gap * gap, 0.0)
            distance = jnp.sum(gap, axis=0, keepdims=True)
            limit = value[3:4, :] + top[3:4, :] + 0.001
            mark[pl.ds(j, 1), :] = jnp.where(
                live & (distance <= limit * limit), 1.0, 0.0
            )
        return carry

    lax.fori_loop(0, total // step, near, 0)
    lane = lax.broadcasted_iota(jnp.int32, (G, G), 1)
    sub = lax.broadcasted_iota(jnp.int32, (G, G), 0)
    upper = (sub <= lane).astype(jnp.bfloat16)
    start = 0
    crowded = []
    for kind, size in enumerate(sizes):
        if not size:
            continue
        if kind == 3:
            keys[start : start + size, :] = lax.broadcasted_iota(
                jnp.int32, (size, G), 1
            ).astype(jnp.float32)
        else:
            held = mark[start : start + size, :]
            rank = jnp.dot(
                held.astype(jnp.bfloat16), upper, preferred_element_type=jnp.float32
            )
            keys[start : start + size, :] = jnp.where(held > 0.0, rank - 1.0, -1.0)
            crowded.append((kind, start, size, jnp.max(rank) > 8.0 * CHUNKS[kind]))
        start += size

    def job(j, chunk_list):
        t, n = tab[j * 5], tab[j * 5 + 1]
        target = block(t_ref, t)
        other = block(n_ref, n)
        target = [target[c : c + 1, :] for c in range(4)]
        other = [other[c : c + 1, :] for c in range(4)]
        key = row(keys, j)
        force = None
        for base in chunk_list:
            part = chunk_force(key, base, other, target)
            force = part if force is None else [x + y for x, y in zip(force, part)]
        for c in range(3):
            here = pl.ds(pl.multiple_of(t * 3 + 8 * c, 8), 8)
            acc[here, :] = acc[here, :] + force[c]

    start = 0
    for kind, size in enumerate(sizes):
        if not size:
            continue
        unroll = UNROLL[kind]

        def body(i, carry, start=start, kind=kind, unroll=unroll):
            for u in range(unroll):
                job(start + i * unroll + u, [8.0 * c for c in range(CHUNKS[kind])])
            return carry

        lax.fori_loop(0, size // unroll, body, 0)
        start += size

    for kind, start, size, over in crowded:

        @pl.when(over)
        def _(kind=kind, start=start, size=size):
            def rest(j, carry):
                def one(c, inner):
                    job(start + j, [8.0 * c.astype(jnp.float32)])
                    return inner

                return lax.fori_loop(CHUNKS[kind], 16, one, carry)

            lax.fori_loop(0, size, rest, 0)


def bounds(st_ref, low, high):
    for t in range(TILES):
        value = st_ref[8 * t : 8 * t + 8, :]
        low[8 * t : 8 * t + 8, :] = jnp.broadcast_to(
            jnp.min(value, axis=1, keepdims=True), (8, G)
        )
        high[8 * t : 8 * t + 8, :] = jnp.broadcast_to(
            jnp.max(value, axis=1, keepdims=True), (8, G)
        )


def settle(acc):
    rows = []
    for t in range(TILES):
        for c in range(3):
            at = 24 * t + 8 * c
            rows.append(jnp.sum(acc[at : at + 8, :], axis=0, keepdims=True))
    return rows


def contact_kernel(sizes, tab_c, st, ret, rel, before, after, total, *scr):
    low, high, mark, keys, acc = scr
    acc[...] = jnp.zeros_like(acc)
    bounds(st, low, high)
    run_contacts(sizes, tab_c, st, st, ret, rel, ret, rel, low, high, mark, keys, None, acc)
    rows = settle(acc)
    for t in range(TILES):
        at = 8 * t
        total[at : at + 8, :] = jnp.zeros((8, G), jnp.float32) if before is None else before[at : at + 8, :]
        for c in range(3):
            total[at + c : at + c + 1, :] = total[at + c : at + c + 1, :] + rows[3 * t + c]


def bridge_kernel(count, tab_b, live, st, part, ret, rel, before, after, total, fresh, *scr):
    *bridge, acc_a, acc_b, jobs = scr
    acc_a[...] = before[...]
    acc_b[...] = jnp.zeros_like(acc_b)
    fresh[...] = jnp.zeros_like(fresh)
    batches = compact(count, lambda j: live[tab_b[j * 5 + 2]], jobs)
    run_bridges(batches, jobs, tab_b, st, st, part, ret, rel, bridge, acc_a, acc_b, fresh)
    for t in range(TILES):
        at = 8 * t
        total[at : at + 4, :] = (
            acc_a[at : at + 4, :] + acc_b[at : at + 4, :] + acc_b[at + 4 : at + 8, :]
        )
        total[at + 4 : at + 8, :] = jnp.zeros((4, G), jnp.float32)


def halo_kernel(
    sizes, n_out, n_in, tab_o, tab_i, tab_c, live, st, part, ret, rel, held, before,
    za, zb, ya, yb, xa, xb, forces, film, fresh, *scr
):
    *bridge, acc_a, acc_b, low, high, mark, keys, seen, acc, halo, flag, jobs_o, jobs_i, flags, sems = scr
    copies = []
    for k, (pair, axis, at, rows) in enumerate(
        (((za, zb), "gz", Z_AT, Z_ROWS), ((ya, yb), "gy", Y_AT, Y_ROWS), ((xa, xb), "gx", X_AT, X_ROWS))
    ):
        odd = lax.axis_index(axis) % 2
        for w, src in enumerate(pair):
            side = (1 - odd) if w == 0 else odd
            copy = pltpu.make_async_copy(
                src, halo.at[pl.ds(at + side * rows, rows), :], sems.at[2 * k + w]
            )
            copy.start()
            copies.append(copy)
    keep = pltpu.make_async_copy(before, fresh, sems.at[6])
    keep.start()
    acc_a[...] = held[...]
    acc_b[...] = jnp.zeros_like(acc_b)
    acc[...] = jnp.zeros_like(acc)
    halo[ZERO_AT : ZERO_AT + 8, :] = jnp.zeros((8, G), jnp.float32)
    bounds(st, low, high)
    out_batches = compact(n_out, lambda j: live[tab_o[j * 5 + 2]], jobs_o)
    for copy in copies:
        copy.wait()
    keep.wait()
    run_contacts(sizes, tab_c, st, halo, ret, rel, halo, halo, low, high, mark, keys, seen, acc)
    first = (
        lax.broadcasted_iota(jnp.int32, (8, G), 0) + lax.broadcasted_iota(jnp.int32, (8, G), 1)
    ) == 0
    listed = lax.dot_general(
        first.astype(jnp.bfloat16),
        (seen[...] > 0.0).astype(jnp.bfloat16),
        (((1,), (1,)), ((), ())),
        preferred_element_type=jnp.float32,
    )
    for k in range(4):
        flag[k : k + 1, :] = listed[0:1, k * G : k * G + G].astype(jnp.int32)
    down = pltpu.make_async_copy(flag, flags, sems.at[7])
    down.start()
    run_bridges(out_batches, jobs_o, tab_o, st, halo, part, ret, rel, bridge, acc_a, None, fresh)
    down.wait()
    in_batches = compact(n_in, lambda j: flags[j // G, j % G], jobs_i)
    run_bridges(in_batches, jobs_i, tab_i, halo, st, halo, halo, halo, bridge, None, acc_b, None)
    rows = settle(acc)
    for t in range(TILES):
        at = 8 * t
        value = acc_a[at : at + 4, :] + acc_b[at : at + 4, :] + acc_b[at + 4 : at + 8, :]
        for c in range(3):
            forces[c, t : t + 1, :] = value[c : c + 1, :] + rows[3 * t + c]
        film[t : t + 1, :] = value[3:4, :] + st[at + 4 : at + 5, :]


def send_sides(axis):
    odd = lax.axis_index(axis) % 2
    return 1 - odd, odd


def own_slots(refs, at):
    return [ref[pl.ds(at, 9), :].astype(jnp.float32) for ref in refs]


def pack_z_kernel(pos, rad, film, part, ret, rel, st, out_a, out_b):
    for g in range(TILES // 8):
        members = [pos[c, 8 * g : 8 * g + 8, :] for c in range(3)]
        members += [rad[8 * g : 8 * g + 8, :], film[8 * g : 8 * g + 8, :]]
        for c, value in enumerate(members):
            st[pl.ds(64 * g + c, 8, stride=8), :] = value
        for c in range(5, 8):
            st[pl.ds(64 * g + c, 8, stride=8), :] = jnp.zeros((8, G), jnp.float32)
    for out, side in zip((out_a, out_b), send_sides("gz")):
        for xy in range(16):
            t = 2 * xy + side
            at = 32 * xy
            out[at : at + 5, :] = st[pl.ds(8 * t, 5), :]
            for k, ref in enumerate((part, ret, rel)):
                rows = ref[pl.ds(27 * t + 2 * side, 9, stride=3), :]
                out[at + 5 + 9 * k : at + 14 + 9 * k, :] = rows.astype(jnp.float32)


def load_sides(pair, axis, buf, rows, sems, first):
    odd = lax.axis_index(axis) % 2
    copies = []
    for w, src in enumerate(pair):
        side = (1 - odd) if w == 0 else odd
        copy = pltpu.make_async_copy(src, buf.at[pl.ds(side * rows, rows), :], sems.at[first + w])
        copy.start()
        copies.append(copy)
    return copies


def pack_y_kernel(st, part, ret, rel, za, zb, after, out_a, out_b, zbuf, sems):
    for copy in load_sides((za, zb), "gz", zbuf, Z_ROWS, sems, 0):
        copy.wait()
    for out, side in zip((out_a, out_b), send_sides("gy")):
        for x in range(4):
            for z in range(2):
                t = tile_number(x, 3 * side, z)
                at = 32 * (2 * x + z)
                out[at : at + 5, :] = st[pl.ds(8 * t, 5), :]
                for k, ref in enumerate((part, ret, rel)):
                    for i in range(3):
                        here = at + 5 + 9 * k + 3 * i
                        rows = ref[pl.ds(27 * t + 9 * i + 6 * side, 3), :]
                        out[here : here + 3, :] = rows.astype(jnp.float32)
        for sz in range(2):
            for x in range(4):
                at = 256 + 16 * (4 * sz + x)
                src = sz * Z_ROWS + (x * 4 + 3 * side) * 32
                out[at : at + 5, :] = zbuf[pl.ds(src, 5), :]
                for k in range(3):
                    out[at + 5 + 3 * k : at + 8 + 3 * k, :] = zbuf[
                        pl.ds(src + 5 + 9 * k + 2 * side, 3, stride=3), :
                    ]
                out[at + 14 : at + 16, :] = jnp.zeros((2, G), jnp.float32)


def pack_x_kernel(st, part, ret, rel, za, zb, ya, yb, after, out_a, out_b, zbuf, ybuf, sems):
    copies = load_sides((za, zb), "gz", zbuf, Z_ROWS, sems, 0)
    copies += load_sides((ya, yb), "gy", ybuf, Y_ROWS, sems, 2)
    for copy in copies:
        copy.wait()
    for out, side in zip((out_a, out_b), send_sides("gx")):
        for y in range(4):
            for z in range(2):
                t = tile_number(3 * side, y, z)
                at = 32 * (2 * y + z)
                out[at : at + 5, :] = st[pl.ds(8 * t, 5), :]
                for k, ref in enumerate((part, ret, rel)):
                    rows = ref[pl.ds(27 * t + 18 * side, 9), :]
                    out[at + 5 + 9 * k : at + 14 + 9 * k, :] = rows.astype(jnp.float32)
        for sy in range(2):
            for z in range(2):
                at = 256 + 16 * (2 * sy + z)
                src = sy * Y_ROWS + (2 * 3 * side + z) * 32
                out[at : at + 5, :] = ybuf[pl.ds(src, 5), :]
                for k in range(3):
                    out[at + 5 + 3 * k : at + 8 + 3 * k, :] = ybuf[
                        pl.ds(src + 5 + 9 * k + 6 * side, 3), :
                    ]
                out[at + 14 : at + 16, :] = jnp.zeros((2, G), jnp.float32)
        for sz in range(2):
            for y in range(4):
                at = 320 + 16 * (4 * sz + y)
                src = sz * Z_ROWS + (4 * 3 * side + y) * 32
                out[at : at + 5, :] = zbuf[pl.ds(src, 5), :]
                for k in range(3):
                    out[at + 5 + 3 * k : at + 8 + 3 * k, :] = zbuf[
                        pl.ds(src + 5 + 9 * k + 6 * side, 3), :
                    ]
                out[at + 14 : at + 16, :] = jnp.zeros((2, G), jnp.float32)
        for sy in range(2):
            for sz in range(2):
                at = 448 + 8 * (2 * sy + sz)
                src = sy * Y_ROWS + 256 + 16 * (4 * sz + 3 * side)
                out[at : at + 5, :] = ybuf[pl.ds(src, 5), :]
                for k in range(3):
                    out[at + 5 + k : at + 6 + k, :] = ybuf[
                        pl.ds(src + 5 + 3 * k + 2 * side, 1), :
                    ]


VM = pl.BlockSpec(memory_space=pltpu.VMEM)
SM = pl.BlockSpec(memory_space=pltpu.SMEM)
AN = pl.BlockSpec(memory_space=pl.ANY)
PARAMS = pltpu.CompilerParams(vmem_limit_bytes=48 * 1024 * 1024)


def rows_of(n):
    return jax.ShapeDtypeStruct((n, G), jnp.float32)


def swap(pair, axis):
    count = lax.axis_size(axis)
    first, second = pair
    near = [(i, i ^ 1) for i in range(count) if i ^ 1 < count]
    far = [(i, ((i + 1) ^ 1) - 1) for i in range(1, count) if ((i + 1) ^ 1) - 1 < count]
    return lax.ppermute(first, axis, near), lax.ppermute(second, axis, far)


def bridge_scratch():
    return [
        pltpu.VMEM((8 * BATCH, G), jnp.float32),
        pltpu.VMEM((8 * BATCH, G), jnp.float32),
        pltpu.VMEM((BATCH, G), jnp.float32),
        pltpu.VMEM((BATCH, G), jnp.float32),
        pltpu.VMEM((8 * BATCH, G), jnp.float32),
        pltpu.VMEM((8 * BATCH, G), jnp.float32),
    ]


def tiles_scratch(count):
    return [pltpu.VMEM((8 * TILES, G), jnp.float32)] * count


def contact_scratch(jobs, halo):
    out = tiles_scratch(2) + [pltpu.VMEM((jobs, G), jnp.float32)] * 2
    if halo:
        out = out + [pltpu.VMEM((512, G), jnp.float32)]
    return out + [pltpu.VMEM((24 * TILES, G), jnp.float32)]


def shards(positions, grain_radii, film_liquid, pair_live, partner, rupture, volume):
    pos = positions.reshape(3, TILES, G)
    rad = grain_radii.reshape(TILES, G)
    film = film_liquid.reshape(TILES, G)
    part = partner.reshape(SLOTS, G)
    vol = volume.reshape(SLOTS, G)
    live = pair_live.reshape(SLOTS, 1) > 0
    broken = rupture.reshape(SLOTS, G) > 0
    ret = jnp.where(live & ~broken, vol, 0.0)
    rel = jnp.where(live & broken, vol, 0.0)

    st, za, zb = pl.pallas_call(
        pack_z_kernel,
        out_shape=(rows_of(8 * TILES), rows_of(Z_ROWS), rows_of(Z_ROWS)),
        in_specs=[VM] * 6,
        out_specs=(VM,) * 3,
        compiler_params=PARAMS,
        name="pack_z",
    )(pos, rad, film, part, ret, rel)
    zero = SLOTS
    extra = jnp.zeros((8, G), jnp.float32)
    part_pad = jnp.concatenate([part, jnp.zeros((8, G), jnp.int32)], axis=0)
    ret_pad = jnp.concatenate([ret, extra], axis=0)
    rel_pad = jnp.concatenate([rel, extra], axis=0)
    flags = pair_live.reshape(SLOTS)

    def contacts(kinds, before, after, name):
        near = contact_tables(False)
        near = [
            pad(near[k], UNROLL[k], (0, 0, zero, zero, zero)) if k in kinds else [] for k in range(4)
        ]
        sizes = tuple(len(rows) for rows in near)
        body = contact_kernel
        if before is None:
            body = lambda sizes, tab, st, ret, rel, after, *rest: contact_kernel(
                sizes, tab, st, ret, rel, None, after, *rest
            )
        given = [] if before is None else [before]
        return pl.pallas_call(
            functools.partial(body, sizes),
            out_shape=rows_of(8 * TILES),
            in_specs=[SM] + [VM] * (3 + len(given)) + [AN],
            out_specs=VM,
            scratch_shapes=contact_scratch(sum(sizes), False),
            compiler_params=PARAMS,
            name=name,
        )(flat(sum(near, [])), st, ret_pad, rel_pad, *given, after)

    inner, outward, inward = bridge_tables()
    dummy = (0, 0, zero, zero, zero)
    za, zb = swap((za, zb), "gz")
    held = contacts((3, 1), None, st, "contact_own")
    ya, yb = pl.pallas_call(
        pack_y_kernel,
        out_shape=(rows_of(Y_ROWS),) * 2,
        in_specs=[VM] * 4 + [AN] * 3,
        out_specs=(VM,) * 2,
        scratch_shapes=[pltpu.VMEM((2 * Z_ROWS, G), jnp.float32), pltpu.SemaphoreType.DMA((2,))],
        compiler_params=PARAMS,
        name="pack_y",
    )(st, part, ret, rel, za, zb, held)
    ya, yb, order_y = *swap((ya, yb), "gy"), ya
    held, fresh = pl.pallas_call(
        functools.partial(bridge_kernel, len(inner)),
        out_shape=(rows_of(8 * TILES), rows_of(SLOTS + 8)),
        in_specs=[SM] * 2 + [VM] * 5 + [AN],
        out_specs=(VM,) * 2,
        scratch_shapes=bridge_scratch()
        + tiles_scratch(2)
        + [pltpu.SMEM((len(inner) + BATCH,), jnp.int32)],
        compiler_params=PARAMS,
        name="bridge_own",
    )(flat(inner + [dummy]), flags, st, part_pad, ret_pad, rel_pad, held, order_y)
    xa, xb = pl.pallas_call(
        pack_x_kernel,
        out_shape=(rows_of(X_ROWS),) * 2,
        in_specs=[VM] * 4 + [AN] * 5,
        out_specs=(VM,) * 2,
        scratch_shapes=[
            pltpu.VMEM((2 * Z_ROWS, G), jnp.float32),
            pltpu.VMEM((2 * Y_ROWS, G), jnp.float32),
            pltpu.SemaphoreType.DMA((4,)),
        ],
        compiler_params=PARAMS,
        name="pack_x",
    )(st, part, ret, rel, za, zb, ya, yb, held)
    xa, xb, order_x = *swap((xa, xb), "gx"), xa
    held = contacts((0, 2), held, order_x, "contact_near")

    far = contact_tables(True)
    far = [pad(rows, UNROLL[k], (0, 0, zero, ZERO_AT, ZERO_AT)) for k, rows in enumerate(far)]
    sizes = tuple(len(rows) for rows in far)
    forces, film_next, fresh = pl.pallas_call(
        functools.partial(halo_kernel, sizes, len(outward), len(inward)),
        out_shape=(
            jax.ShapeDtypeStruct((3, TILES, G), jnp.float32),
            rows_of(TILES),
            rows_of(SLOTS + 8),
        ),
        in_specs=[SM] * 4 + [VM] * 5 + [AN] * 7,
        out_specs=(VM,) * 3,
        scratch_shapes=bridge_scratch()
        + tiles_scratch(2)
        + contact_scratch(sum(sizes), True)
        + [
            pltpu.VMEM((HALO_ROWS, G), jnp.float32),
            pltpu.VMEM((8, G), jnp.int32),
            pltpu.SMEM((len(outward) + BATCH,), jnp.int32),
            pltpu.SMEM((len(inward) + BATCH,), jnp.int32),
            pltpu.SMEM((8, G), jnp.int32),
            pltpu.SemaphoreType.DMA((8,)),
        ],
        compiler_params=PARAMS,
        name="halo",
    )(
        flat(outward + [dummy]),
        flat(inward + [(0, 0, ZERO_AT, ZERO_AT, ZERO_AT)]),
        flat(sum(far, [])),
        flags, st, part_pad, ret_pad, rel_pad, held, fresh, za, zb, ya, yb, xa, xb,
    )
    return (
        forces.reshape(positions.shape),
        film_next.reshape(film_liquid.shape),
        fresh[:SLOTS].reshape(volume.shape),
    )


def solution(mesh):
    return jax.shard_map(
        shards,
        mesh=mesh,
        in_specs=(
            P(None, "gx", "gy", "gz", None),
            P("gx", "gy", "gz", None),
            P("gx", "gy", "gz", None),
            P("gx", "gy", "gz", None),
            P("gx", "gy", "gz", None, None),
            P("gx", "gy", "gz", None, None),
            P("gx", "gy", "gz", None, None),
        ),
        out_specs=(
            P(None, "gx", "gy", "gz", None),
            P("gx", "gy", "gz", None),
            P("gx", "gy", "gz", None, None),
        ),
        check_vma=False,
    )
```

```python
import functools

import jax
import jax.numpy as jnp
import numpy as np
from jax import lax
from jax.experimental import pallas as pl
from jax.experimental.pallas import tpu as pltpu
from jax.sharding import PartitionSpec as P

ABSORB = 0.02
BX, BY, BZ = 4, 4, 2
TILES = BX * BY * BZ
SLOTS = 27 * TILES
G = 128
Z_ROWS = 16 * 32
Y_ROWS = 8 * 32 + 8 * 16
X_ROWS = 8 * 32 + 4 * 16 + 8 * 16 + 4 * 8
Z_AT = 0
Y_AT = 2 * Z_ROWS
X_AT = Y_AT + 2 * Y_ROWS
ZERO_AT = X_AT + 2 * X_ROWS
HALO_ROWS = ZERO_AT + 8
BATCH = 64
OFFSETS = [(i, j, k) for i in (-1, 0, 1) for j in (-1, 0, 1) for k in (-1, 0, 1)]


def tile_number(x, y, z):
    return (x * BY + y) * BZ + z


def code(e):
    return 9 * (e[0] + 1) + 3 * (e[1] + 1) + e[2] + 1


def inside(x, y, z):
    return 0 <= x < BX and 0 <= y < BY and 0 <= z < BZ


def halo_block(x, y, z):
    side = lambda v: 0 if v < 0 else 1
    ox, oy, oz = not 0 <= x < BX, not 0 <= y < BY, not 0 <= z < BZ
    if ox:
        base = X_AT + side(x) * X_ROWS
        if oy and oz:
            return base + 448 + (side(y) * 2 + side(z)) * 8, 1
        if oy:
            return base + 256 + (side(y) * 2 + z) * 16, 3
        if oz:
            return base + 320 + (side(z) * 4 + y) * 16, 3
        return base + (y * 2 + z) * 32, 9
    if oy:
        base = Y_AT + side(y) * Y_ROWS
        if oz:
            return base + 256 + (side(z) * 4 + x) * 16, 3
        return base + (x * 2 + z) * 32, 9
    return Z_AT + side(z) * Z_ROWS + (x * 4 + y) * 32, 9


def halo_slot(x, y, z, e):
    base, count = halo_block(x, y, z)
    free = [v + 1 for v, c, n in zip(e, (x, y, z), (BX, BY, BZ)) if 0 <= c < n]
    k = 0
    for v in free:
        k = 3 * k + v
    return base + 5 + k, base + 5 + count + k, base + 5 + 2 * count + k


def pairs():
    for x in range(BX):
        for y in range(BY):
            for z in range(BZ):
                for e in OFFSETS:
                    yield (x, y, z), e, (x + e[0], y + e[1], z + e[2])


def pad(rows, multiple, dummy):
    rows = list(rows)
    while len(rows) % multiple:
        rows.append(dummy)
    return rows


def bridge_tables():
    inner, outward, inward = [], [], [[], [], [], []]
    for t, e, b in pairs():
        own = 8 * tile_number(*t)
        s = 27 * tile_number(*t) + code(e)
        if inside(*b):
            inner.append((own, 8 * tile_number(*b), s, s, s))
        else:
            back = tuple(-v for v in e)
            outward.append((own, halo_block(*b)[0], s, s, s))
            inward[contact_class(e)].append((halo_block(*b)[0], own) + halo_slot(*b, back))
    return inner, outward, sum(inward, [])


def contact_class(e):
    kinds = sum(abs(v) for v in e)
    if kinds == 0:
        return 3
    if kinds > 1:
        return 0
    return 1 if e[0] else 2


CHUNKS = (1, 2, 4, 16)
UNROLL = (80, 16, 16, 4)


def contact_tables(halo):
    out = [[], [], [], []]
    for t, e, b in pairs():
        own = 8 * tile_number(*t)
        s = 27 * tile_number(*t) + code(e)
        back = tuple(-v for v in e)
        kind = contact_class(e)
        if inside(*b):
            s2 = 27 * tile_number(*b) + code(back)
            if not halo:
                out[kind].append((own, 8 * tile_number(*b), s, s2, s2))
        elif halo:
            _, ret, rel = halo_slot(*b, back)
            out[kind].append((own, halo_block(*b)[0], s, ret, rel))
    return out


def flat(rows):
    return np.asarray(rows, np.int32).reshape(-1)


def row(ref, at):
    return ref[pl.ds(at, 1), :]


def block(ref, at):
    return ref[pl.ds(pl.multiple_of(at, 8), 8), :]


class Listing:
    def __init__(self, count, listed, jobs):
        self.count, self.listed, self.jobs = count, listed, jobs

    def share(self, i, steps, n):
        each = -(-self.count // steps)
        assert each * steps == self.count
        for u in range(each):
            j = i * each + u
            self.jobs[n] = j
            n = n + self.listed(j)
        return n

    def close(self, n):
        for u in range(BATCH):
            self.jobs[n + u] = self.count
        return (n + BATCH - 1) // BATCH


def run_bridges(batches, jobs, tab, a_ref, b_ref, p_ref, q_ref, l_ref, scr, acc_a, acc_b, next_ref):
    m_ref, a_scr, q_scr, l_scr, f_ref, g_ref = scr

    def body(i, carry):
        at = []
        for j in range(BATCH):
            o = jobs[i * BATCH + j] * 5
            at.append([tab[o + k] for k in range(5)])
        partner = []
        for j in range(BATCH):
            a, b, p, q, l = at[j]
            idx = row(p_ref, p).astype(jnp.int32)
            m_ref[8 * j : 8 * j + 8, :] = jnp.take_along_axis(
                block(b_ref, b), jnp.broadcast_to(idx, (8, G)), axis=1
            )
            a_scr[8 * j : 8 * j + 8, :] = block(a_ref, a)
            q_scr[j : j + 1, :] = row(q_ref, q)
            l_scr[j : j + 1, :] = row(l_ref, l)
        for g in range(BATCH // 8):
            near = [m_ref[pl.ds(64 * g + c, 8, stride=8), :] for c in range(5)]
            own = [a_scr[pl.ds(64 * g + c, 8, stride=8), :] for c in range(5)]
            held = q_scr[8 * g : 8 * g + 8, :]
            half = 0.5 * l_scr[8 * g : 8 * g + 8, :]
            gap = [own[c] - near[c] for c in range(3)]
            squares = gap[0] * gap[0] + gap[1] * gap[1] + gap[2] * gap[2]
            inverse = lax.rsqrt(squares)
            spacing = squares * inverse
            radius_sum = own[3] + near[3]
            harmonic = 2.0 * own[3] * near[3] / radius_sum
            scaled = (
                jnp.maximum(spacing - radius_sum, 0.0) * harmonic * lax.rsqrt(harmonic * held)
            )
            intact = held > 0.0
            tension = harmonic * inverse / (1.0 + 1.05 * scaled + 2.5 * scaled * scaled)
            tension = jnp.where(intact, tension, 0.0)
            absorb = jnp.where(intact, ABSORB, 0.0)
            force = [tension * gap[c] for c in range(3)]
            if acc_b is not None:
                for c, value in enumerate(force + [half - absorb * near[4]]):
                    high = value.astype(jnp.bfloat16).astype(jnp.float32)
                    f_ref[pl.ds(64 * g + c, 8, stride=8), :] = high
                    f_ref[pl.ds(64 * g + 4 + c, 8, stride=8), :] = value - high
            if acc_a is not None:
                for c in range(3):
                    g_ref[pl.ds(64 * g + c, 8, stride=8), :] = -force[c]
                g_ref[pl.ds(64 * g + 3, 8, stride=8), :] = half - absorb * own[4]
                g_ref[pl.ds(64 * g + 4, 8, stride=8), :] = jnp.where(
                    intact, held + ABSORB * (own[4] + near[4]), 0.0
                )
        if acc_a is not None:
            for j in range(BATCH):
                a, b, p, q, l = at[j]
                here = pl.ds(pl.multiple_of(a, 8), 8)
                acc_a[here, :] = acc_a[here, :] + g_ref[8 * j : 8 * j + 8, :]
                next_ref[pl.ds(p, 1), :] = g_ref[8 * j + 4 : 8 * j + 5, :]
        if acc_b is not None:
            sub = lax.broadcasted_iota(jnp.int32, (G, G), 0)
            none = jnp.zeros((8, G), jnp.float32)
            for j in range(0, BATCH, 2):
                left, choose = [], []
                for h in range(2):
                    idx = row(p_ref, at[j + h][2]).astype(jnp.int32)
                    choose.append((sub == idx).astype(jnp.bfloat16))
                    value = f_ref[8 * (j + h) : 8 * (j + h) + 8, :]
                    left.append(jnp.concatenate([none] * h + [value] + [none] * (1 - h), axis=1))
                landed = lax.dot_general(
                    jnp.concatenate(left, axis=0).astype(jnp.bfloat16),
                    jnp.concatenate(choose, axis=1),
                    (((1,), (1,)), ((), ())),
                    preferred_element_type=jnp.float32,
                )
                for h in range(2):
                    here = pl.ds(pl.multiple_of(at[j + h][1], 8), 8)
                    acc_b[here, :] = acc_b[here, :] + landed[8 * h : 8 * h + 8, :]
        return carry

    lax.fori_loop(0, batches, body, 0)


def chunk_force(key, base, other, target):
    sub = lax.broadcasted_iota(jnp.int32, (8, G), 0).astype(jnp.float32) + base
    chosen = key == sub
    rows = [
        jnp.sum(jnp.where(chosen, other[c], 0.0), axis=1, keepdims=True) for c in range(4)
    ]
    radius = jnp.where(rows[3] > 0.0, rows[3], -1000.0)
    delta = [target[c] - rows[c] for c in range(3)]
    squares = delta[0] * delta[0] + delta[1] * delta[1] + delta[2] * delta[2]
    squares = jnp.maximum(squares, 1e-6)
    inverse = lax.rsqrt(squares)
    reach = target[3] + radius
    overlap = jnp.maximum(reach - squares * inverse, 0.0)
    weight = target[3] * radius * overlap
    push = overlap * inverse * weight * lax.rsqrt(jnp.maximum(weight * reach, 1e-30))
    return [push * delta[c] for c in range(3)]


def run_contacts(sizes, tab, t_ref, n_ref, q_ref, l_ref, nq_ref, nl_ref, low, high, mark, keys, seen, acc, beside=()):
    beside = dict(beside)
    lists = {}
    total = sum(sizes)
    step = max(k for k in range(1, 81) if total % k == 0)
    wide = lax.broadcasted_iota(jnp.int32, (8, G), 0)

    def near(i, carry):
        for u in range(step):
            j = i * step + u
            t, n, s, nq, nl = [tab[j * 5 + k] for k in range(5)]
            theirs = row(nq_ref, nq) + row(nl_ref, nl)
            if seen is not None:
                seen[pl.ds(j, 1), :] = theirs
            live = row(q_ref, s) + row(l_ref, s) + theirs > 0.0
            value = block(n_ref, n)
            top = block(high, t)
            gap = jnp.maximum(jnp.maximum(block(low, t) - value, value - top), 0.0)
            gap = jnp.where(wide < 3, gap * gap, 0.0)
            distance = jnp.sum(gap, axis=0, keepdims=True)
            limit = value[3:4, :] + top[3:4, :] + 0.001
            mark[pl.ds(j, 1), :] = jnp.where(
                live & (distance <= limit * limit), 1.0, 0.0
            )
        if "near" in beside:
            carry = beside["near"].share(i, total // step, carry)
        return carry

    n = lax.fori_loop(0, total // step, near, 0)
    if "near" in beside:
        lists["near"] = beside["near"].close(n)
    if "marked" in beside:
        beside["marked"]()
    lane = lax.broadcasted_iota(jnp.int32, (G, G), 1)
    sub = lax.broadcasted_iota(jnp.int32, (G, G), 0)
    upper = (sub <= lane).astype(jnp.bfloat16)
    start = 0
    crowded = []
    for kind, size in enumerate(sizes):
        if not size:
            continue
        if kind == 3:
            keys[start : start + size, :] = lax.broadcasted_iota(
                jnp.int32, (size, G), 1
            ).astype(jnp.float32)
        else:
            held = mark[start : start + size, :]
            rank = jnp.dot(
                held.astype(jnp.bfloat16), upper, preferred_element_type=jnp.float32
            )
            keys[start : start + size, :] = jnp.where(held > 0.0, rank - 1.0, -1.0)
            crowded.append((kind, start, size, jnp.max(rank) > 8.0 * CHUNKS[kind]))
        start += size

    def job(j, chunk_list):
        t, n = tab[j * 5], tab[j * 5 + 1]
        target = block(t_ref, t)
        other = block(n_ref, n)
        target = [target[c : c + 1, :] for c in range(4)]
        other = [other[c : c + 1, :] for c in range(4)]
        key = row(keys, j)
        force = None
        for base in chunk_list:
            part = chunk_force(key, base, other, target)
            force = part if force is None else [x + y for x, y in zip(force, part)]
        for c in range(3):
            here = pl.ds(pl.multiple_of(t * 3 + 8 * c, 8), 8)
            acc[here, :] = acc[here, :] + force[c]

    start = 0
    for kind, size in enumerate(sizes):
        if not size:
            continue
        unroll = UNROLL[kind]

        def body(i, carry, start=start, kind=kind, unroll=unroll):
            for u in range(unroll):
                job(start + i * unroll + u, [8.0 * c for c in range(CHUNKS[kind])])
            if kind in beside:
                carry = beside[kind].share(i, size // unroll, carry)
            return carry

        if kind in beside and "ready" in beside:
            beside["ready"]()
        n = lax.fori_loop(0, size // unroll, body, 0)
        if kind in beside:
            lists[kind] = beside[kind].close(n)
        start += size

    for kind, start, size, over in crowded:

        @pl.when(over)
        def _(kind=kind, start=start, size=size):
            def rest(j, carry):
                def one(c, inner):
                    job(start + j, [8.0 * c.astype(jnp.float32)])
                    return inner

                return lax.fori_loop(CHUNKS[kind], 16, one, carry)

            lax.fori_loop(0, size, rest, 0)

    return lists


def bounds(st_ref, low, high):
    for t in range(TILES):
        value = st_ref[8 * t : 8 * t + 8, :]
        low[8 * t : 8 * t + 8, :] = jnp.broadcast_to(
            jnp.min(value, axis=1, keepdims=True), (8, G)
        )
        high[8 * t : 8 * t + 8, :] = jnp.broadcast_to(
            jnp.max(value, axis=1, keepdims=True), (8, G)
        )


def settle(acc):
    rows = []
    for t in range(TILES):
        for c in range(3):
            at = 24 * t + 8 * c
            rows.append(jnp.sum(acc[at : at + 8, :], axis=0, keepdims=True))
    return rows


def first_kernel(sizes, tab_c, st, ret, rel, after, low, high, acc, mark, keys):
    acc[...] = jnp.zeros_like(acc)
    bounds(st, low, high)
    run_contacts(sizes, tab_c, st, st, ret, rel, ret, rel, low, high, mark, keys, None, acc)


def bridge_kernel(
    sizes, count, tab_c, tab_b, live, st, part, ret, rel, low, high, before, after,
    acc, acc_a, fresh, *scr
):
    *bridge, acc_b, mark, keys, jobs = scr
    acc[...] = before[...]
    acc_a[...] = jnp.zeros_like(acc_a)
    acc_b[...] = jnp.zeros_like(acc_b)
    fresh[...] = jnp.zeros_like(fresh)
    listing = Listing(count, lambda j: live[tab_b[j * 5 + 2]], jobs)
    lists = run_contacts(
        sizes, tab_c, st, st, ret, rel, ret, rel, low, high, mark, keys, None, acc,
        beside={3: listing},
    )
    run_bridges(lists[3], jobs, tab_b, st, st, part, ret, rel, bridge, acc_a, acc_b, fresh)
    for t in range(TILES):
        at = 8 * t
        acc_a[at : at + 4, :] = (
            acc_a[at : at + 4, :] + acc_b[at : at + 4, :] + acc_b[at + 4 : at + 8, :]
        )


def third_kernel(sizes, tab_c, st, ret, rel, low, high, before, after, acc, mark, keys):
    acc[...] = before[...]
    run_contacts(sizes, tab_c, st, st, ret, rel, ret, rel, low, high, mark, keys, None, acc)


def halo_kernel(
    sizes, n_out, n_in, tab_o, tab_i, tab_c, live, st, part, ret, rel, low, high, held, pushed,
    before, za, zb, ya, yb, xa, xb, forces, film, fresh, *scr
):
    (*bridge, acc_a, acc_b, mark, keys, seen, acc, halo, store, flag, jobs_o, jobs_i, flags, sems) = scr
    copies = []
    for k, (pair, axis, at, rows) in enumerate(
        (((za, zb), "gz", Z_AT, Z_ROWS), ((ya, yb), "gy", Y_AT, Y_ROWS), ((xa, xb), "gx", X_AT, X_ROWS))
    ):
        odd = lax.axis_index(axis) % 2
        for w, src in enumerate(pair):
            side = (1 - odd) if w == 0 else odd
            copy = pltpu.make_async_copy(
                src, halo.at[pl.ds(at + side * rows, rows), :], sems.at[2 * k + w]
            )
            copy.start()
            copies.append(copy)
    keep = pltpu.make_async_copy(before, store, sems.at[6])
    keep.start()
    acc_a[...] = held[...]
    acc_b[...] = jnp.zeros_like(acc_b)
    acc[...] = pushed[...]
    halo[ZERO_AT : ZERO_AT + 8, :] = jnp.zeros((8, G), jnp.float32)
    seen[sum(sizes) :, :] = jnp.zeros((512 - sum(sizes), G), jnp.float32)
    for copy in copies:
        copy.wait()
    down = pltpu.make_async_copy(flag, flags, sems.at[7])

    def marked():
        first = (
            lax.broadcasted_iota(jnp.int32, (8, G), 0) + lax.broadcasted_iota(jnp.int32, (8, G), 1)
        ) == 0
        listed = lax.dot_general(
            first.astype(jnp.bfloat16),
            (seen[...] > 0.0).astype(jnp.bfloat16),
            (((1,), (1,)), ((), ())),
            preferred_element_type=jnp.float32,
        )
        for k in range(4):
            flag[k : k + 1, :] = listed[0:1, k * G : k * G + G].astype(jnp.int32)
        down.start()

    lists = run_contacts(
        sizes, tab_c, st, halo, ret, rel, halo, halo, low, high, mark, keys, seen, acc,
        beside={
            "near": Listing(n_out, lambda j: live[tab_o[j * 5 + 2]], jobs_o),
            "marked": marked,
            "ready": down.wait,
            0: Listing(n_in, lambda j: flags[j // G, j % G], jobs_i),
        },
    )
    keep.wait()
    run_bridges(lists["near"], jobs_o, tab_o, st, halo, part, ret, rel, bridge, acc_a, None, store)
    leave = pltpu.make_async_copy(store.at[pl.ds(0, SLOTS), :], fresh, sems.at[6])
    leave.start()
    run_bridges(lists[0], jobs_i, tab_i, halo, st, halo, halo, halo, bridge, None, acc_b, None)
    rows = settle(acc)
    for t in range(TILES):
        at = 8 * t
        value = acc_a[at : at + 4, :] + acc_b[at : at + 4, :] + acc_b[at + 4 : at + 8, :]
        for c in range(3):
            forces[c, t : t + 1, :] = value[c : c + 1, :] + rows[3 * t + c]
        film[t : t + 1, :] = value[3:4, :] + st[at + 4 : at + 5, :]
    leave.wait()


def send_sides(axis):
    odd = lax.axis_index(axis) % 2
    return 1 - odd, odd


def own_slots(refs, at):
    return [ref[pl.ds(at, 9), :].astype(jnp.float32) for ref in refs]


def pack_z_kernel(pos, rad, film, part, ret, rel, st, out_a, out_b):
    for g in range(TILES // 8):
        members = [pos[c, 8 * g : 8 * g + 8, :] for c in range(3)]
        members += [rad[8 * g : 8 * g + 8, :], film[8 * g : 8 * g + 8, :]]
        for c, value in enumerate(members):
            st[pl.ds(64 * g + c, 8, stride=8), :] = value
        for c in range(5, 8):
            st[pl.ds(64 * g + c, 8, stride=8), :] = jnp.zeros((8, G), jnp.float32)
    for out, side in zip((out_a, out_b), send_sides("gz")):
        for xy in range(16):
            t = 2 * xy + side
            at = 32 * xy
            out[at : at + 5, :] = st[pl.ds(8 * t, 5), :]
            for k, ref in enumerate((part, ret, rel)):
                rows = ref[pl.ds(27 * t + 2 * side, 9, stride=3), :]
                out[at + 5 + 9 * k : at + 14 + 9 * k, :] = rows.astype(jnp.float32)


def load_sides(pair, axis, buf, rows, sems, first):
    odd = lax.axis_index(axis) % 2
    copies = []
    for w, src in enumerate(pair):
        side = (1 - odd) if w == 0 else odd
        copy = pltpu.make_async_copy(src, buf.at[pl.ds(side * rows, rows), :], sems.at[first + w])
        copy.start()
        copies.append(copy)
    return copies


def pack_y_kernel(st, part, ret, rel, za, zb, after, out_a, out_b, zbuf, sems):
    for copy in load_sides((za, zb), "gz", zbuf, Z_ROWS, sems, 0):
        copy.wait()
    for out, side in zip((out_a, out_b), send_sides("gy")):
        for x in range(4):
            for z in range(2):
                t = tile_number(x, 3 * side, z)
                at = 32 * (2 * x + z)
                out[at : at + 5, :] = st[pl.ds(8 * t, 5), :]
                for k, ref in enumerate((part, ret, rel)):
                    for i in range(3):
                        here = at + 5 + 9 * k + 3 * i
                        rows = ref[pl.ds(27 * t + 9 * i + 6 * side, 3), :]
                        out[here : here + 3, :] = rows.astype(jnp.float32)
        for sz in range(2):
            for x in range(4):
                at = 256 + 16 * (4 * sz + x)
                src = sz * Z_ROWS + (x * 4 + 3 * side) * 32
                out[at : at + 5, :] = zbuf[pl.ds(src, 5), :]
                for k in range(3):
                    out[at + 5 + 3 * k : at + 8 + 3 * k, :] = zbuf[
                        pl.ds(src + 5 + 9 * k + 2 * side, 3, stride=3), :
                    ]
                out[at + 14 : at + 16, :] = jnp.zeros((2, G), jnp.float32)


def pack_x_kernel(st, part, ret, rel, za, zb, ya, yb, after, out_a, out_b, zbuf, ybuf, sems):
    copies = load_sides((za, zb), "gz", zbuf, Z_ROWS, sems, 0)
    copies += load_sides((ya, yb), "gy", ybuf, Y_ROWS, sems, 2)
    for copy in copies:
        copy.wait()
    for out, side in zip((out_a, out_b), send_sides("gx")):
        for y in range(4):
            for z in range(2):
                t = tile_number(3 * side, y, z)
                at = 32 * (2 * y + z)
                out[at : at + 5, :] = st[pl.ds(8 * t, 5), :]
                for k, ref in enumerate((part, ret, rel)):
                    rows = ref[pl.ds(27 * t + 18 * side, 9), :]
                    out[at + 5 + 9 * k : at + 14 + 9 * k, :] = rows.astype(jnp.float32)
        for sy in range(2):
            for z in range(2):
                at = 256 + 16 * (2 * sy + z)
                src = sy * Y_ROWS + (2 * 3 * side + z) * 32
                out[at : at + 5, :] = ybuf[pl.ds(src, 5), :]
                for k in range(3):
                    out[at + 5 + 3 * k : at + 8 + 3 * k, :] = ybuf[
                        pl.ds(src + 5 + 9 * k + 6 * side, 3), :
                    ]
                out[at + 14 : at + 16, :] = jnp.zeros((2, G), jnp.float32)
        for sz in range(2):
            for y in range(4):
                at = 320 + 16 * (4 * sz + y)
                src = sz * Z_ROWS + (4 * 3 * side + y) * 32
                out[at : at + 5, :] = zbuf[pl.ds(src, 5), :]
                for k in range(3):
                    out[at + 5 + 3 * k : at + 8 + 3 * k, :] = zbuf[
                        pl.ds(src + 5 + 9 * k + 6 * side, 3), :
                    ]
                out[at + 14 : at + 16, :] = jnp.zeros((2, G), jnp.float32)
        for sy in range(2):
            for sz in range(2):
                at = 448 + 8 * (2 * sy + sz)
                src = sy * Y_ROWS + 256 + 16 * (4 * sz + 3 * side)
                out[at : at + 5, :] = ybuf[pl.ds(src, 5), :]
                for k in range(3):
                    out[at + 5 + k : at + 6 + k, :] = ybuf[
                        pl.ds(src + 5 + 3 * k + 2 * side, 1), :
                    ]


VM = pl.BlockSpec(memory_space=pltpu.VMEM)
SM = pl.BlockSpec(memory_space=pltpu.SMEM)
AN = pl.BlockSpec(memory_space=pl.ANY)
PARAMS = pltpu.CompilerParams(vmem_limit_bytes=48 * 1024 * 1024)


def rows_of(n):
    return jax.ShapeDtypeStruct((n, G), jnp.float32)


def swap(pair, axis):
    count = lax.axis_size(axis)
    first, second = pair
    near = [(i, i ^ 1) for i in range(count) if i ^ 1 < count]
    far = [(i, ((i + 1) ^ 1) - 1) for i in range(1, count) if ((i + 1) ^ 1) - 1 < count]
    return lax.ppermute(first, axis, near), lax.ppermute(second, axis, far)


def bridge_scratch():
    return [
        pltpu.VMEM((8 * BATCH, G), jnp.float32),
        pltpu.VMEM((8 * BATCH, G), jnp.float32),
        pltpu.VMEM((BATCH, G), jnp.float32),
        pltpu.VMEM((BATCH, G), jnp.float32),
        pltpu.VMEM((8 * BATCH, G), jnp.float32),
        pltpu.VMEM((8 * BATCH, G), jnp.float32),
    ]


def tiles_scratch(count):
    return [pltpu.VMEM((8 * TILES, G), jnp.float32)] * count


def contact_scratch(jobs):
    return [pltpu.VMEM((jobs, G), jnp.float32)] * 2


def shards(positions, grain_radii, film_liquid, pair_live, partner, rupture, volume):
    pos = positions.reshape(3, TILES, G)
    rad = grain_radii.reshape(TILES, G)
    film = film_liquid.reshape(TILES, G)
    part = partner.reshape(SLOTS, G)
    vol = volume.reshape(SLOTS, G)
    live = pair_live.reshape(SLOTS, 1) > 0
    broken = rupture.reshape(SLOTS, G) > 0
    ret = jnp.where(live & ~broken, vol, 0.0)
    rel = jnp.where(live & broken, vol, 0.0)

    st, za, zb = pl.pallas_call(
        pack_z_kernel,
        out_shape=(rows_of(8 * TILES), rows_of(Z_ROWS), rows_of(Z_ROWS)),
        in_specs=[VM] * 6,
        out_specs=(VM,) * 3,
        compiler_params=PARAMS,
        name="pack_z",
    )(pos, rad, film, part, ret, rel)
    zero = SLOTS
    extra = jnp.zeros((8, G), jnp.float32)
    part_pad = jnp.concatenate([part, jnp.zeros((8, G), jnp.int32)], axis=0)
    ret_pad = jnp.concatenate([ret, extra], axis=0)
    rel_pad = jnp.concatenate([rel, extra], axis=0)
    flags = pair_live.reshape(SLOTS)

    def near_jobs(kinds):
        near = contact_tables(False)
        near = [
            pad(near[k], UNROLL[k], (0, 0, zero, zero, zero)) if k in kinds else [] for k in range(4)
        ]
        return tuple(len(rows) for rows in near), flat(sum(near, []))

    inner, outward, inward = bridge_tables()
    dummy = (0, 0, zero, zero, zero)
    sums = rows_of(24 * TILES)
    tile_rows = rows_of(8 * TILES)
    za, zb = swap((za, zb), "gz")
    sizes, tab = near_jobs((0, 1))
    low, high, pushed = pl.pallas_call(
        functools.partial(first_kernel, sizes),
        out_shape=(tile_rows, tile_rows, sums),
        in_specs=[SM] + [VM] * 3 + [AN],
        out_specs=(VM,) * 3,
        scratch_shapes=contact_scratch(sum(sizes)),
        compiler_params=PARAMS,
        name="first",
    )(tab, st, ret_pad, rel_pad, st)
    ya, yb = pl.pallas_call(
        pack_y_kernel,
        out_shape=(rows_of(Y_ROWS),) * 2,
        in_specs=[VM] * 4 + [AN] * 3,
        out_specs=(VM,) * 2,
        scratch_shapes=[pltpu.VMEM((2 * Z_ROWS, G), jnp.float32), pltpu.SemaphoreType.DMA((2,))],
        compiler_params=PARAMS,
        name="pack_y",
    )(st, part, ret, rel, za, zb, pushed)
    order_y = ya
    ya, yb = swap((ya, yb), "gy")
    sizes, tab = near_jobs((3,))
    pushed, held, fresh = pl.pallas_call(
        functools.partial(bridge_kernel, sizes, len(inner)),
        out_shape=(sums, tile_rows, rows_of(SLOTS + 8)),
        in_specs=[SM] * 3 + [VM] * 7 + [AN],
        out_specs=(VM,) * 3,
        scratch_shapes=bridge_scratch()
        + tiles_scratch(1)
        + contact_scratch(sum(sizes))
        + [pltpu.SMEM((len(inner) + BATCH,), jnp.int32)],
        compiler_params=PARAMS,
        name="bridge_own",
    )(tab, flat(inner + [dummy]), flags, st, part_pad, ret_pad, rel_pad, low, high, pushed, order_y)
    xa, xb = pl.pallas_call(
        pack_x_kernel,
        out_shape=(rows_of(X_ROWS),) * 2,
        in_specs=[VM] * 4 + [AN] * 5,
        out_specs=(VM,) * 2,
        scratch_shapes=[
            pltpu.VMEM((2 * Z_ROWS, G), jnp.float32),
            pltpu.VMEM((2 * Y_ROWS, G), jnp.float32),
            pltpu.SemaphoreType.DMA((4,)),
        ],
        compiler_params=PARAMS,
        name="pack_x",
    )(st, part, ret, rel, za, zb, ya, yb, held)
    order_x = xa
    xa, xb = swap((xa, xb), "gx")
    sizes, tab = near_jobs((2,))
    pushed = pl.pallas_call(
        functools.partial(third_kernel, sizes),
        out_shape=sums,
        in_specs=[SM] + [VM] * 6 + [AN],
        out_specs=VM,
        scratch_shapes=contact_scratch(sum(sizes)),
        compiler_params=PARAMS,
        name="third",
    )(tab, st, ret_pad, rel_pad, low, high, pushed, order_x)

    far = contact_tables(True)
    far = [pad(rows, UNROLL[k], (0, 0, zero, ZERO_AT, ZERO_AT)) for k, rows in enumerate(far)]
    sizes = tuple(len(rows) for rows in far)
    inward = pad(inward, 5, (0, 0, ZERO_AT, ZERO_AT, ZERO_AT))
    forces, film_next, fresh = pl.pallas_call(
        functools.partial(halo_kernel, sizes, len(outward), len(inward)),
        out_shape=(
            jax.ShapeDtypeStruct((3, TILES, G), jnp.float32),
            rows_of(TILES),
            rows_of(SLOTS),
        ),
        in_specs=[SM] * 4 + [VM] * 8 + [AN] * 7,
        out_specs=(VM, VM, AN),
        scratch_shapes=bridge_scratch()
        + tiles_scratch(2)
        + contact_scratch(sum(sizes))
        + [
            pltpu.VMEM((512, G), jnp.float32),
            pltpu.VMEM((24 * TILES, G), jnp.float32),
            pltpu.VMEM((HALO_ROWS, G), jnp.float32),
            pltpu.VMEM((SLOTS + 8, G), jnp.float32),
            pltpu.VMEM((8, G), jnp.int32),
            pltpu.SMEM((len(outward) + BATCH,), jnp.int32),
            pltpu.SMEM((len(inward) + BATCH,), jnp.int32),
            pltpu.SMEM((8, G), jnp.int32),
            pltpu.SemaphoreType.DMA((8,)),
        ],
        compiler_params=PARAMS,
        name="halo",
    )(
        flat(outward + [dummy]),
        flat(inward + [(0, 0, ZERO_AT, ZERO_AT, ZERO_AT)]),
        flat(sum(far, [])),
        flags, st, part_pad, ret_pad, rel_pad, low, high, held, pushed, fresh,
        za, zb, ya, yb, xa, xb,
    )
    return (
        forces.reshape(positions.shape),
        film_next.reshape(film_liquid.shape),
        fresh.reshape(volume.shape),
    )


def solution(mesh):
    return jax.shard_map(
        shards,
        mesh=mesh,
        in_specs=(
            P(None, "gx", "gy", "gz", None),
            P("gx", "gy", "gz", None),
            P("gx", "gy", "gz", None),
            P("gx", "gy", "gz", None),
            P("gx", "gy", "gz", None, None),
            P("gx", "gy", "gz", None, None),
            P("gx", "gy", "gz", None, None),
        ),
        out_specs=(
            P(None, "gx", "gy", "gz", None),
            P("gx", "gy", "gz", None),
            P("gx", "gy", "gz", None, None),
        ),
        check_vma=False,
    )
```

```python
import functools

import jax
import jax.numpy as jnp
import numpy as np
from jax import lax
from jax.experimental import pallas as pl
from jax.experimental.pallas import tpu as pltpu
from jax.sharding import PartitionSpec as P

ABSORB = 0.02
BX, BY, BZ = 4, 4, 2
TILES = BX * BY * BZ
SLOTS = 27 * TILES
G = 128
Z_ROWS = 16 * 32
Y_ROWS = 8 * 32 + 8 * 16
X_ROWS = 8 * 32 + 4 * 16 + 8 * 16 + 4 * 8
Z_AT = 0
Y_AT = 2 * Z_ROWS
X_AT = Y_AT + 2 * Y_ROWS
ZERO_AT = X_AT + 2 * X_ROWS
HALO_ROWS = ZERO_AT + 8
BATCH = 64
OFFSETS = [(i, j, k) for i in (-1, 0, 1) for j in (-1, 0, 1) for k in (-1, 0, 1)]


def tile_number(x, y, z):
    return (x * BY + y) * BZ + z


def code(e):
    return 9 * (e[0] + 1) + 3 * (e[1] + 1) + e[2] + 1


def inside(x, y, z):
    return 0 <= x < BX and 0 <= y < BY and 0 <= z < BZ


def halo_block(x, y, z):
    side = lambda v: 0 if v < 0 else 1
    ox, oy, oz = not 0 <= x < BX, not 0 <= y < BY, not 0 <= z < BZ
    if ox:
        base = X_AT + side(x) * X_ROWS
        if oy and oz:
            return base + 448 + (side(y) * 2 + side(z)) * 8, 1
        if oy:
            return base + 256 + (side(y) * 2 + z) * 16, 3
        if oz:
            return base + 320 + (side(z) * 4 + y) * 16, 3
        return base + (y * 2 + z) * 32, 9
    if oy:
        base = Y_AT + side(y) * Y_ROWS
        if oz:
            return base + 256 + (side(z) * 4 + x) * 16, 3
        return base + (x * 2 + z) * 32, 9
    return Z_AT + side(z) * Z_ROWS + (x * 4 + y) * 32, 9


def halo_slot(x, y, z, e):
    base, count = halo_block(x, y, z)
    free = [v + 1 for v, c, n in zip(e, (x, y, z), (BX, BY, BZ)) if 0 <= c < n]
    k = 0
    for v in free:
        k = 3 * k + v
    return base + 5 + k, base + 5 + count + k, base + 5 + 2 * count + k


def pairs():
    for x in range(BX):
        for y in range(BY):
            for z in range(BZ):
                for e in OFFSETS:
                    yield (x, y, z), e, (x + e[0], y + e[1], z + e[2])


def pad(rows, multiple, dummy):
    rows = list(rows)
    while len(rows) % multiple:
        rows.append(dummy)
    return rows


def bridge_tables():
    inner, outward, inward = [], [], [[], [], [], []]
    for t, e, b in pairs():
        own = 8 * tile_number(*t)
        s = 27 * tile_number(*t) + code(e)
        if inside(*b):
            inner.append((own, 8 * tile_number(*b), s, s, s))
        else:
            back = tuple(-v for v in e)
            outward.append((own, halo_block(*b)[0], s, s, s))
            inward[contact_class(e)].append((halo_block(*b)[0], own) + halo_slot(*b, back))
    return inner, outward, sum(inward, [])


def contact_class(e):
    kinds = sum(abs(v) for v in e)
    if kinds == 0:
        return 3
    if kinds > 1:
        return 0
    return 1 if e[0] else 2


CHUNKS = (1, 2, 4, 16)
UNROLL = (80, 16, 16, 4)


def contact_tables(halo):
    out = [[], [], [], []]
    for t, e, b in pairs():
        own = 8 * tile_number(*t)
        s = 27 * tile_number(*t) + code(e)
        back = tuple(-v for v in e)
        kind = contact_class(e)
        if inside(*b):
            s2 = 27 * tile_number(*b) + code(back)
            if not halo:
                out[kind].append((own, 8 * tile_number(*b), s, s2, s2))
        elif halo:
            _, ret, rel = halo_slot(*b, back)
            out[kind].append((own, halo_block(*b)[0], s, ret, rel))
    return out


def flat(rows):
    return np.asarray(rows, np.int32).reshape(-1)


def row(ref, at):
    return ref[pl.ds(at, 1), :]


def block(ref, at):
    return ref[pl.ds(pl.multiple_of(at, 8), 8), :]


class Listing:
    def __init__(self, count, listed, jobs):
        self.count, self.listed, self.jobs = count, listed, jobs

    def share(self, i, steps, n):
        each = -(-self.count // steps)
        assert each * steps == self.count
        for u in range(each):
            j = i * each + u
            self.jobs[n] = j
            n = n + self.listed(j)
        return n

    def close(self, n):
        for u in range(BATCH):
            self.jobs[n + u] = self.count
        return (n + BATCH - 1) // BATCH


def run_bridges(batches, jobs, tab, a_ref, b_ref, p_ref, q_ref, l_ref, scr, acc_a, acc_b, next_ref):
    m_ref, a_scr, q_scr, l_scr, f_ref, g_ref = scr

    def body(i, carry):
        at = []
        for j in range(BATCH):
            o = jobs[i * BATCH + j] * 5
            at.append([tab[o + k] for k in range(5)])
        partner = []
        for j in range(BATCH):
            a, b, p, q, l = at[j]
            idx = row(p_ref, p).astype(jnp.int32)
            m_ref[8 * j : 8 * j + 8, :] = jnp.take_along_axis(
                block(b_ref, b), jnp.broadcast_to(idx, (8, G)), axis=1
            )
            a_scr[8 * j : 8 * j + 8, :] = block(a_ref, a)
            q_scr[j : j + 1, :] = row(q_ref, q)
            l_scr[j : j + 1, :] = row(l_ref, l)
        for g in range(BATCH // 8):
            near = [m_ref[pl.ds(64 * g + c, 8, stride=8), :] for c in range(5)]
            own = [a_scr[pl.ds(64 * g + c, 8, stride=8), :] for c in range(5)]
            held = q_scr[8 * g : 8 * g + 8, :]
            half = 0.5 * l_scr[8 * g : 8 * g + 8, :]
            gap = [own[c] - near[c] for c in range(3)]
            squares = gap[0] * gap[0] + gap[1] * gap[1] + gap[2] * gap[2]
            inverse = lax.rsqrt(squares)
            spacing = squares * inverse
            radius_sum = own[3] + near[3]
            harmonic = 2.0 * own[3] * near[3] / radius_sum
            scaled = (
                jnp.maximum(spacing - radius_sum, 0.0) * harmonic * lax.rsqrt(harmonic * held)
            )
            intact = held > 0.0
            tension = harmonic * inverse / (1.0 + 1.05 * scaled + 2.5 * scaled * scaled)
            tension = jnp.where(intact, tension, 0.0)
            absorb = jnp.where(intact, ABSORB, 0.0)
            force = [tension * gap[c] for c in range(3)]
            if acc_b is not None:
                for c, value in enumerate(force + [half - absorb * near[4]]):
                    high = value.astype(jnp.bfloat16).astype(jnp.float32)
                    f_ref[pl.ds(64 * g + c, 8, stride=8), :] = high
                    f_ref[pl.ds(64 * g + 4 + c, 8, stride=8), :] = value - high
            if acc_a is not None:
                for c in range(3):
                    g_ref[pl.ds(64 * g + c, 8, stride=8), :] = -force[c]
                g_ref[pl.ds(64 * g + 3, 8, stride=8), :] = half - absorb * own[4]
                g_ref[pl.ds(64 * g + 4, 8, stride=8), :] = jnp.where(
                    intact, held + ABSORB * (own[4] + near[4]), 0.0
                )
        if acc_a is not None:
            for j in range(BATCH):
                a, b, p, q, l = at[j]
                here = pl.ds(pl.multiple_of(a, 8), 8)
                acc_a[here, :] = acc_a[here, :] + g_ref[8 * j : 8 * j + 8, :]
                next_ref[pl.ds(q, 1), :] = g_ref[8 * j + 4 : 8 * j + 5, :]
        if acc_b is not None:
            sub = lax.broadcasted_iota(jnp.int32, (G, G), 0)
            none = jnp.zeros((8, G), jnp.float32)
            for j in range(0, BATCH, 2):
                left, choose = [], []
                for h in range(2):
                    idx = row(p_ref, at[j + h][2]).astype(jnp.int32)
                    choose.append((sub == idx).astype(jnp.bfloat16))
                    value = f_ref[8 * (j + h) : 8 * (j + h) + 8, :]
                    left.append(jnp.concatenate([none] * h + [value] + [none] * (1 - h), axis=1))
                landed = lax.dot_general(
                    jnp.concatenate(left, axis=0).astype(jnp.bfloat16),
                    jnp.concatenate(choose, axis=1),
                    (((1,), (1,)), ((), ())),
                    preferred_element_type=jnp.float32,
                )
                for h in range(2):
                    here = pl.ds(pl.multiple_of(at[j + h][1], 8), 8)
                    acc_b[here, :] = acc_b[here, :] + landed[8 * h : 8 * h + 8, :]
        return carry

    lax.fori_loop(0, batches, body, 0)


def chunk_force(key, base, other, target):
    sub = lax.broadcasted_iota(jnp.int32, (8, G), 0).astype(jnp.float32) + base
    chosen = key == sub
    rows = [
        jnp.sum(jnp.where(chosen, other[c], 0.0), axis=1, keepdims=True) for c in range(4)
    ]
    radius = jnp.where(rows[3] > 0.0, rows[3], -1000.0)
    delta = [target[c] - rows[c] for c in range(3)]
    squares = delta[0] * delta[0] + delta[1] * delta[1] + delta[2] * delta[2]
    squares = jnp.maximum(squares, 1e-6)
    inverse = lax.rsqrt(squares)
    reach = target[3] + radius
    overlap = jnp.maximum(reach - squares * inverse, 0.0)
    weight = target[3] * radius * overlap
    push = overlap * inverse * weight * lax.rsqrt(jnp.maximum(weight * reach, 1e-30))
    return [push * delta[c] for c in range(3)]


def run_contacts(sizes, tab, t_ref, n_ref, q_ref, l_ref, nq_ref, nl_ref, low, high, mark, keys, seen, acc, beside=()):
    beside = dict(beside)
    lists = {}
    total = sum(sizes)
    step = max(k for k in range(1, 81) if total % k == 0)
    wide = lax.broadcasted_iota(jnp.int32, (8, G), 0)

    def near(i, carry):
        for u in range(step):
            j = i * step + u
            t, n, s, nq, nl = [tab[j * 5 + k] for k in range(5)]
            theirs = row(nq_ref, nq) + row(nl_ref, nl)
            if seen is not None:
                seen[pl.ds(j, 1), :] = theirs
            live = row(q_ref, s) + row(l_ref, s) + theirs > 0.0
            value = block(n_ref, n)
            top = block(high, t)
            gap = jnp.maximum(jnp.maximum(block(low, t) - value, value - top), 0.0)
            gap = jnp.where(wide < 3, gap * gap, 0.0)
            distance = jnp.sum(gap, axis=0, keepdims=True)
            limit = value[3:4, :] + top[3:4, :] + 0.001
            mark[pl.ds(j, 1), :] = jnp.where(
                live & (distance <= limit * limit), 1.0, 0.0
            )
        if "near" in beside:
            carry = beside["near"].share(i, total // step, carry)
        return carry

    n = lax.fori_loop(0, total // step, near, 0)
    if "near" in beside:
        lists["near"] = beside["near"].close(n)
    if "marked" in beside:
        beside["marked"]()
    lane = lax.broadcasted_iota(jnp.int32, (G, G), 1)
    sub = lax.broadcasted_iota(jnp.int32, (G, G), 0)
    upper = (sub <= lane).astype(jnp.bfloat16)
    start = 0
    crowded = []
    for kind, size in enumerate(sizes):
        if not size:
            continue
        if kind == 3:
            keys[start : start + size, :] = lax.broadcasted_iota(
                jnp.int32, (size, G), 1
            ).astype(jnp.float32)
        else:
            held = mark[start : start + size, :]
            rank = jnp.dot(
                held.astype(jnp.bfloat16), upper, preferred_element_type=jnp.float32
            )
            keys[start : start + size, :] = jnp.where(held > 0.0, rank - 1.0, -1.0)
            crowded.append((kind, start, size, jnp.max(rank) > 8.0 * CHUNKS[kind]))
        start += size

    def job(j, chunk_list):
        t, n = tab[j * 5], tab[j * 5 + 1]
        target = block(t_ref, t)
        other = block(n_ref, n)
        target = [target[c : c + 1, :] for c in range(4)]
        other = [other[c : c + 1, :] for c in range(4)]
        key = row(keys, j)
        force = None
        for base in chunk_list:
            part = chunk_force(key, base, other, target)
            force = part if force is None else [x + y for x, y in zip(force, part)]
        for c in range(3):
            here = pl.ds(pl.multiple_of(t * 3 + 8 * c, 8), 8)
            acc[here, :] = acc[here, :] + force[c]

    start = 0
    for kind, size in enumerate(sizes):
        if not size:
            continue
        unroll = UNROLL[kind]

        def body(i, carry, start=start, kind=kind, unroll=unroll):
            for u in range(unroll):
                job(start + i * unroll + u, [8.0 * c for c in range(CHUNKS[kind])])
            if kind in beside:
                carry = beside[kind].share(i, size // unroll, carry)
            return carry

        if kind in beside and "ready" in beside:
            beside["ready"]()
        n = lax.fori_loop(0, size // unroll, body, 0)
        if kind in beside:
            lists[kind] = beside[kind].close(n)
        start += size

    for kind, start, size, over in crowded:

        @pl.when(over)
        def _(kind=kind, start=start, size=size):
            def rest(j, carry):
                def one(c, inner):
                    job(start + j, [8.0 * c.astype(jnp.float32)])
                    return inner

                return lax.fori_loop(CHUNKS[kind], 16, one, carry)

            lax.fori_loop(0, size, rest, 0)

    return lists


def bounds(st_ref, low, high):
    for t in range(TILES):
        value = st_ref[8 * t : 8 * t + 8, :]
        low[8 * t : 8 * t + 8, :] = jnp.broadcast_to(
            jnp.min(value, axis=1, keepdims=True), (8, G)
        )
        high[8 * t : 8 * t + 8, :] = jnp.broadcast_to(
            jnp.max(value, axis=1, keepdims=True), (8, G)
        )


def settle(acc):
    rows = []
    for t in range(TILES):
        for c in range(3):
            at = 24 * t + 8 * c
            rows.append(jnp.sum(acc[at : at + 8, :], axis=0, keepdims=True))
    return rows


def first_kernel(sizes, tab_c, st, ret, rel, after, low, high, acc, mark, keys):
    acc[...] = jnp.zeros_like(acc)
    bounds(st, low, high)
    run_contacts(sizes, tab_c, st, st, ret, rel, ret, rel, low, high, mark, keys, None, acc)


def bridge_kernel(
    sizes, count, tab_c, tab_b, live, st, part, ret, rel, low, high, before, after,
    acc, acc_a, fresh, *scr
):
    *bridge, acc_b, mark, keys, jobs = scr
    acc[...] = before[...]
    acc_a[...] = jnp.zeros_like(acc_a)
    acc_b[...] = jnp.zeros_like(acc_b)
    fresh[...] = jnp.zeros_like(fresh)
    listing = Listing(count, lambda j: live[tab_b[j * 5 + 2]], jobs)
    lists = run_contacts(
        sizes, tab_c, st, st, ret, rel, ret, rel, low, high, mark, keys, None, acc,
        beside={3: listing},
    )
    run_bridges(lists[3], jobs, tab_b, st, st, part, ret, rel, bridge, acc_a, acc_b, fresh)
    for t in range(TILES):
        at = 8 * t
        acc_a[at : at + 4, :] = (
            acc_a[at : at + 4, :] + acc_b[at : at + 4, :] + acc_b[at + 4 : at + 8, :]
        )


def third_kernel(sizes, tab_c, st, ret, rel, low, high, before, after, acc, mark, keys):
    acc[...] = before[...]
    run_contacts(sizes, tab_c, st, st, ret, rel, ret, rel, low, high, mark, keys, None, acc)


def halo_kernel(
    sizes, n_out, n_in, tab_o, tab_i, tab_c, live, st, part, ret, rel, low, high, held, pushed,
    before, za, zb, ya, yb, xa, xb, forces, film, fresh, *scr
):
    (*bridge, acc_a, acc_b, mark, keys, seen, acc, halo, store, flag, jobs_o, jobs_i, flags, sems) = scr
    copies = []
    for k, (pair, axis, at, rows) in enumerate(
        (((za, zb), "gz", Z_AT, Z_ROWS), ((ya, yb), "gy", Y_AT, Y_ROWS), ((xa, xb), "gx", X_AT, X_ROWS))
    ):
        odd = lax.axis_index(axis) % 2
        for w, src in enumerate(pair):
            side = (1 - odd) if w == 0 else odd
            copy = pltpu.make_async_copy(
                src, halo.at[pl.ds(at + side * rows, rows), :], sems.at[2 * k + w]
            )
            copy.start()
            copies.append(copy)
    keep = pltpu.make_async_copy(before, store, sems.at[6])
    keep.start()
    acc_a[...] = held[...]
    acc_b[...] = jnp.zeros_like(acc_b)
    acc[...] = pushed[...]
    halo[ZERO_AT : ZERO_AT + 8, :] = jnp.zeros((8, G), jnp.float32)
    seen[sum(sizes) :, :] = jnp.zeros((512 - sum(sizes), G), jnp.float32)
    for copy in copies:
        copy.wait()
    down = pltpu.make_async_copy(flag, flags, sems.at[7])

    def marked():
        first = (
            lax.broadcasted_iota(jnp.int32, (8, G), 0) + lax.broadcasted_iota(jnp.int32, (8, G), 1)
        ) == 0
        listed = lax.dot_general(
            first.astype(jnp.bfloat16),
            (seen[...] > 0.0).astype(jnp.bfloat16),
            (((1,), (1,)), ((), ())),
            preferred_element_type=jnp.float32,
        )
        for k in range(4):
            flag[k : k + 1, :] = listed[0:1, k * G : k * G + G].astype(jnp.int32)
        down.start()

    lists = run_contacts(
        sizes, tab_c, st, halo, ret, rel, halo, halo, low, high, mark, keys, seen, acc,
        beside={
            "near": Listing(n_out, lambda j: live[tab_o[j * 5 + 2]], jobs_o),
            "marked": marked,
            "ready": down.wait,
            0: Listing(n_in, lambda j: flags[j // G, j % G], jobs_i),
        },
    )
    keep.wait()
    run_bridges(lists["near"], jobs_o, tab_o, st, halo, part, ret, rel, bridge, acc_a, None, store)
    leave = pltpu.make_async_copy(store.at[pl.ds(0, SLOTS), :], fresh, sems.at[6])
    leave.start()
    run_bridges(lists[0], jobs_i, tab_i, halo, st, halo, halo, halo, bridge, None, acc_b, None)
    rows = settle(acc)
    for t in range(TILES):
        at = 8 * t
        value = acc_a[at : at + 4, :] + acc_b[at : at + 4, :] + acc_b[at + 4 : at + 8, :]
        for c in range(3):
            forces[c, t : t + 1, :] = value[c : c + 1, :] + rows[3 * t + c]
        film[t : t + 1, :] = value[3:4, :] + st[at + 4 : at + 5, :]
    leave.wait()


def send_sides(axis):
    odd = lax.axis_index(axis) % 2
    return 1 - odd, odd


def own_slots(refs, at):
    return [ref[pl.ds(at, 9), :].astype(jnp.float32) for ref in refs]


def pack_z_kernel(
    pos_in, rad_in, film_in, live_in, part_in, broken_in, vol_in, st, part, ret, rel, out_a, out_b,
    pos, rad, film, live, broken, vol, sems,
):
    copies = [
        pltpu.make_async_copy(src, dst, sems.at[k])
        for k, (src, dst) in enumerate(
            (
                (live_in, live), (broken_in, broken), (vol_in, vol), (part_in, part),
                (pos_in, pos), (rad_in, rad), (film_in, film),
            )
        )
    ]
    for copy in copies:
        copy.start()
    for copy in copies:
        copy.wait()
    flags = [live[0:1, G * k : G * k + G] for k in range(SLOTS // G)]
    rest = SLOTS - G * (SLOTS // G)
    flags.append(
        jnp.concatenate(
            [live[0:1, SLOTS - rest : SLOTS], jnp.zeros((1, G - rest), jnp.int32)], axis=1
        )
    )
    flags.append(jnp.zeros((8 - len(flags), G), jnp.int32))
    columns = jnp.transpose(jnp.concatenate(flags, axis=0).astype(jnp.float32))
    for k in range(SLOTS // G + 1):
        count = min(G, SLOTS - G * k)
        here = slice(G * k, G * k + count)
        listed = jnp.broadcast_to(columns[0:count, k : k + 1], (count, G)) > 0.0
        lost = broken[here, :] > 0
        held = jnp.where(listed, vol[here, :], 0.0)
        ret[here, :] = jnp.where(lost, 0.0, held)
        rel[here, :] = jnp.where(lost, held, 0.0)
    for ref in (ret, rel):
        ref[SLOTS : SLOTS + 8, :] = jnp.zeros((8, G), jnp.float32)
    for g in range(TILES // 8):
        members = [pos[c, 8 * g : 8 * g + 8, :] for c in range(3)]
        members += [rad[8 * g : 8 * g + 8, :], film[8 * g : 8 * g + 8, :]]
        for c, value in enumerate(members):
            st[pl.ds(64 * g + c, 8, stride=8), :] = value
        for c in range(5, 8):
            st[pl.ds(64 * g + c, 8, stride=8), :] = jnp.zeros((8, G), jnp.float32)
    for out, side in zip((out_a, out_b), send_sides("gz")):
        for xy in range(16):
            t = 2 * xy + side
            at = 32 * xy
            out[at : at + 5, :] = st[pl.ds(8 * t, 5), :]
            for k, ref in enumerate((part, ret, rel)):
                rows = ref[pl.ds(27 * t + 2 * side, 9, stride=3), :]
                out[at + 5 + 9 * k : at + 14 + 9 * k, :] = rows.astype(jnp.float32)


def load_sides(pair, axis, buf, rows, sems, first):
    odd = lax.axis_index(axis) % 2
    copies = []
    for w, src in enumerate(pair):
        side = (1 - odd) if w == 0 else odd
        copy = pltpu.make_async_copy(src, buf.at[pl.ds(side * rows, rows), :], sems.at[first + w])
        copy.start()
        copies.append(copy)
    return copies


def pack_y_kernel(st, part, ret, rel, za, zb, after, out_a, out_b, zbuf, sems):
    for copy in load_sides((za, zb), "gz", zbuf, Z_ROWS, sems, 0):
        copy.wait()
    for out, side in zip((out_a, out_b), send_sides("gy")):
        for x in range(4):
            for z in range(2):
                t = tile_number(x, 3 * side, z)
                at = 32 * (2 * x + z)
                out[at : at + 5, :] = st[pl.ds(8 * t, 5), :]
                for k, ref in enumerate((part, ret, rel)):
                    for i in range(3):
                        here = at + 5 + 9 * k + 3 * i
                        rows = ref[pl.ds(27 * t + 9 * i + 6 * side, 3), :]
                        out[here : here + 3, :] = rows.astype(jnp.float32)
        for sz in range(2):
            for x in range(4):
                at = 256 + 16 * (4 * sz + x)
                src = sz * Z_ROWS + (x * 4 + 3 * side) * 32
                out[at : at + 5, :] = zbuf[pl.ds(src, 5), :]
                for k in range(3):
                    out[at + 5 + 3 * k : at + 8 + 3 * k, :] = zbuf[
                        pl.ds(src + 5 + 9 * k + 2 * side, 3, stride=3), :
                    ]
                out[at + 14 : at + 16, :] = jnp.zeros((2, G), jnp.float32)


def pack_x_kernel(st, part, ret, rel, za, zb, ya, yb, after, out_a, out_b, zbuf, ybuf, sems):
    copies = load_sides((za, zb), "gz", zbuf, Z_ROWS, sems, 0)
    copies += load_sides((ya, yb), "gy", ybuf, Y_ROWS, sems, 2)
    for copy in copies:
        copy.wait()
    for out, side in zip((out_a, out_b), send_sides("gx")):
        for y in range(4):
            for z in range(2):
                t = tile_number(3 * side, y, z)
                at = 32 * (2 * y + z)
                out[at : at + 5, :] = st[pl.ds(8 * t, 5), :]
                for k, ref in enumerate((part, ret, rel)):
                    rows = ref[pl.ds(27 * t + 18 * side, 9), :]
                    out[at + 5 + 9 * k : at + 14 + 9 * k, :] = rows.astype(jnp.float32)
        for sy in range(2):
            for z in range(2):
                at = 256 + 16 * (2 * sy + z)
                src = sy * Y_ROWS + (2 * 3 * side + z) * 32
                out[at : at + 5, :] = ybuf[pl.ds(src, 5), :]
                for k in range(3):
                    out[at + 5 + 3 * k : at + 8 + 3 * k, :] = ybuf[
                        pl.ds(src + 5 + 9 * k + 6 * side, 3), :
                    ]
                out[at + 14 : at + 16, :] = jnp.zeros((2, G), jnp.float32)
        for sz in range(2):
            for y in range(4):
                at = 320 + 16 * (4 * sz + y)
                src = sz * Z_ROWS + (4 * 3 * side + y) * 32
                out[at : at + 5, :] = zbuf[pl.ds(src, 5), :]
                for k in range(3):
                    out[at + 5 + 3 * k : at + 8 + 3 * k, :] = zbuf[
                        pl.ds(src + 5 + 9 * k + 6 * side, 3), :
                    ]
                out[at + 14 : at + 16, :] = jnp.zeros((2, G), jnp.float32)
        for sy in range(2):
            for sz in range(2):
                at = 448 + 8 * (2 * sy + sz)
                src = sy * Y_ROWS + 256 + 16 * (4 * sz + 3 * side)
                out[at : at + 5, :] = ybuf[pl.ds(src, 5), :]
                for k in range(3):
                    out[at + 5 + k : at + 6 + k, :] = ybuf[
                        pl.ds(src + 5 + 3 * k + 2 * side, 1), :
                    ]


VM = pl.BlockSpec(memory_space=pltpu.VMEM)
SM = pl.BlockSpec(memory_space=pltpu.SMEM)
AN = pl.BlockSpec(memory_space=pl.ANY)
PARAMS = pltpu.CompilerParams(vmem_limit_bytes=48 * 1024 * 1024)


def rows_of(n):
    return jax.ShapeDtypeStruct((n, G), jnp.float32)


def swap(pair, axis):
    count = lax.axis_size(axis)
    first, second = pair
    near = [(i, i ^ 1) for i in range(count) if i ^ 1 < count]
    far = [(i, ((i + 1) ^ 1) - 1) for i in range(1, count) if ((i + 1) ^ 1) - 1 < count]
    return lax.ppermute(first, axis, near), lax.ppermute(second, axis, far)


def bridge_scratch():
    return [
        pltpu.VMEM((8 * BATCH, G), jnp.float32),
        pltpu.VMEM((8 * BATCH, G), jnp.float32),
        pltpu.VMEM((BATCH, G), jnp.float32),
        pltpu.VMEM((BATCH, G), jnp.float32),
        pltpu.VMEM((8 * BATCH, G), jnp.float32),
        pltpu.VMEM((8 * BATCH, G), jnp.float32),
    ]


def tiles_scratch(count):
    return [pltpu.VMEM((8 * TILES, G), jnp.float32)] * count


def contact_scratch(jobs):
    return [pltpu.VMEM((jobs, G), jnp.float32)] * 2


def shards(positions, grain_radii, film_liquid, pair_live, partner, rupture, volume):
    pos = positions.reshape(3, TILES, G)
    rad = grain_radii.reshape(TILES, G)
    film = film_liquid.reshape(TILES, G)
    part = partner.reshape(SLOTS, G)
    vol = volume.reshape(SLOTS, G)
    broken = rupture.reshape(SLOTS, G)

    st, part, ret, rel, za, zb = pl.pallas_call(
        pack_z_kernel,
        out_shape=(
            rows_of(8 * TILES),
            jax.ShapeDtypeStruct((SLOTS, G), jnp.int32),
            rows_of(SLOTS + 8),
            rows_of(SLOTS + 8),
            rows_of(Z_ROWS),
            rows_of(Z_ROWS),
        ),
        in_specs=[pl.BlockSpec(memory_space=pltpu.HBM)] * 7,
        out_specs=(VM,) * 6,
        scratch_shapes=[
            pltpu.VMEM((3, TILES, G), jnp.float32),
            pltpu.VMEM((TILES, G), jnp.float32),
            pltpu.VMEM((TILES, G), jnp.float32),
            pltpu.VMEM((1, SLOTS), jnp.int32),
            pltpu.VMEM((SLOTS, G), jnp.int32),
            pltpu.VMEM((SLOTS, G), jnp.float32),
            pltpu.SemaphoreType.DMA((7,)),
        ],
        compiler_params=PARAMS,
        name="pack_z",
    )(
        *[
            pltpu.with_memory_space_constraint(value, pltpu.HBM)
            for value in (pos, rad, film, pair_live.reshape(1, SLOTS), part, broken, vol)
        ]
    )
    zero = SLOTS
    flags = pair_live.reshape(SLOTS)

    def near_jobs(kinds):
        near = contact_tables(False)
        near = [
            pad(near[k], UNROLL[k], (0, 0, zero, zero, zero)) if k in kinds else [] for k in range(4)
        ]
        return tuple(len(rows) for rows in near), flat(sum(near, []))

    inner, outward, inward = bridge_tables()
    dummy = (0, 0, 0, zero, zero)
    sums = rows_of(24 * TILES)
    tile_rows = rows_of(8 * TILES)
    za, zb = swap((za, zb), "gz")
    sizes, tab = near_jobs((0, 1))
    low, high, pushed = pl.pallas_call(
        functools.partial(first_kernel, sizes),
        out_shape=(tile_rows, tile_rows, sums),
        in_specs=[SM] + [VM] * 3 + [AN],
        out_specs=(VM,) * 3,
        scratch_shapes=contact_scratch(sum(sizes)),
        compiler_params=PARAMS,
        name="first",
    )(tab, st, ret, rel, st)
    ya, yb = pl.pallas_call(
        pack_y_kernel,
        out_shape=(rows_of(Y_ROWS),) * 2,
        in_specs=[VM] * 4 + [AN] * 3,
        out_specs=(VM,) * 2,
        scratch_shapes=[pltpu.VMEM((2 * Z_ROWS, G), jnp.float32), pltpu.SemaphoreType.DMA((2,))],
        compiler_params=PARAMS,
        name="pack_y",
    )(st, part, ret, rel, za, zb, pushed)
    order_y = ya
    ya, yb = swap((ya, yb), "gy")
    sizes, tab = near_jobs((3,))
    pushed, held, fresh = pl.pallas_call(
        functools.partial(bridge_kernel, sizes, len(inner)),
        out_shape=(sums, tile_rows, rows_of(SLOTS + 8)),
        in_specs=[SM] * 3 + [VM] * 7 + [AN],
        out_specs=(VM,) * 3,
        scratch_shapes=bridge_scratch()
        + tiles_scratch(1)
        + contact_scratch(sum(sizes))
        + [pltpu.SMEM((len(inner) + BATCH,), jnp.int32)],
        compiler_params=PARAMS,
        name="bridge_own",
    )(tab, flat(inner + [dummy]), flags, st, part, ret, rel, low, high, pushed, order_y)
    xa, xb = pl.pallas_call(
        pack_x_kernel,
        out_shape=(rows_of(X_ROWS),) * 2,
        in_specs=[VM] * 4 + [AN] * 5,
        out_specs=(VM,) * 2,
        scratch_shapes=[
            pltpu.VMEM((2 * Z_ROWS, G), jnp.float32),
            pltpu.VMEM((2 * Y_ROWS, G), jnp.float32),
            pltpu.SemaphoreType.DMA((4,)),
        ],
        compiler_params=PARAMS,
        name="pack_x",
    )(st, part, ret, rel, za, zb, ya, yb, held)
    order_x = xa
    xa, xb = swap((xa, xb), "gx")
    sizes, tab = near_jobs((2,))
    pushed = pl.pallas_call(
        functools.partial(third_kernel, sizes),
        out_shape=sums,
        in_specs=[SM] + [VM] * 6 + [AN],
        out_specs=VM,
        scratch_shapes=contact_scratch(sum(sizes)),
        compiler_params=PARAMS,
        name="third",
    )(tab, st, ret, rel, low, high, pushed, order_x)

    far = contact_tables(True)
    far = [pad(rows, UNROLL[k], (0, 0, zero, ZERO_AT, ZERO_AT)) for k, rows in enumerate(far)]
    sizes = tuple(len(rows) for rows in far)
    inward = pad(inward, 5, (0, 0, ZERO_AT, ZERO_AT, ZERO_AT))
    forces, film_next, fresh = pl.pallas_call(
        functools.partial(halo_kernel, sizes, len(outward), len(inward)),
        out_shape=(
            jax.ShapeDtypeStruct((3, TILES, G), jnp.float32),
            rows_of(TILES),
            rows_of(SLOTS),
        ),
        in_specs=[SM] * 4 + [VM] * 8 + [AN] * 7,
        out_specs=(VM, VM, AN),
        scratch_shapes=bridge_scratch()
        + tiles_scratch(2)
        + contact_scratch(sum(sizes))
        + [
            pltpu.VMEM((512, G), jnp.float32),
            pltpu.VMEM((24 * TILES, G), jnp.float32),
            pltpu.VMEM((HALO_ROWS, G), jnp.float32),
            pltpu.VMEM((SLOTS + 8, G), jnp.float32),
            pltpu.VMEM((8, G), jnp.int32),
            pltpu.SMEM((len(outward) + BATCH,), jnp.int32),
            pltpu.SMEM((len(inward) + BATCH,), jnp.int32),
            pltpu.SMEM((8, G), jnp.int32),
            pltpu.SemaphoreType.DMA((8,)),
        ],
        compiler_params=PARAMS,
        name="halo",
    )(
        flat(outward + [dummy]),
        flat(inward + [(0, 0, ZERO_AT, ZERO_AT, ZERO_AT)]),
        flat(sum(far, [])),
        flags, st, part, ret, rel, low, high, held, pushed, fresh,
        za, zb, ya, yb, xa, xb,
    )
    return (
        forces.reshape(positions.shape),
        film_next.reshape(film_liquid.shape),
        fresh.reshape(volume.shape),
    )


def solution(mesh):
    return jax.shard_map(
        shards,
        mesh=mesh,
        in_specs=(
            P(None, "gx", "gy", "gz", None),
            P("gx", "gy", "gz", None),
            P("gx", "gy", "gz", None),
            P("gx", "gy", "gz", None),
            P("gx", "gy", "gz", None, None),
            P("gx", "gy", "gz", None, None),
            P("gx", "gy", "gz", None, None),
        ),
        out_specs=(
            P(None, "gx", "gy", "gz", None),
            P("gx", "gy", "gz", None),
            P("gx", "gy", "gz", None, None),
        ),
        check_vma=False,
    )
```

```python
import functools

import jax
import jax.numpy as jnp
import numpy as np
from jax import lax
from jax.experimental import pallas as pl
from jax.experimental.pallas import tpu as pltpu
from jax.sharding import PartitionSpec as P

ABSORB = 0.02
BX, BY, BZ = 4, 4, 2
TILES = BX * BY * BZ
SLOTS = 27 * TILES
G = 128
Z_ROWS = 16 * 32
Y_ROWS = 8 * 32 + 8 * 16
X_ROWS = 8 * 32 + 4 * 16 + 8 * 16 + 4 * 8
Z_AT = 0
Y_AT = 2 * Z_ROWS
X_AT = Y_AT + 2 * Y_ROWS
ZERO_AT = X_AT + 2 * X_ROWS
HALO_ROWS = ZERO_AT + 8
BATCH = 96
OFFSETS = [(i, j, k) for i in (-1, 0, 1) for j in (-1, 0, 1) for k in (-1, 0, 1)]


def tile_number(x, y, z):
    return (x * BY + y) * BZ + z


def code(e):
    return 9 * (e[0] + 1) + 3 * (e[1] + 1) + e[2] + 1


def inside(x, y, z):
    return 0 <= x < BX and 0 <= y < BY and 0 <= z < BZ


def halo_block(x, y, z):
    side = lambda v: 0 if v < 0 else 1
    ox, oy, oz = not 0 <= x < BX, not 0 <= y < BY, not 0 <= z < BZ
    if ox:
        base = X_AT + side(x) * X_ROWS
        if oy and oz:
            return base + 448 + (side(y) * 2 + side(z)) * 8, 1
        if oy:
            return base + 256 + (side(y) * 2 + z) * 16, 3
        if oz:
            return base + 320 + (side(z) * 4 + y) * 16, 3
        return base + (y * 2 + z) * 32, 9
    if oy:
        base = Y_AT + side(y) * Y_ROWS
        if oz:
            return base + 256 + (side(z) * 4 + x) * 16, 3
        return base + (x * 2 + z) * 32, 9
    return Z_AT + side(z) * Z_ROWS + (x * 4 + y) * 32, 9


def halo_slot(x, y, z, e):
    base, count = halo_block(x, y, z)
    free = [v + 1 for v, c, n in zip(e, (x, y, z), (BX, BY, BZ)) if 0 <= c < n]
    k = 0
    for v in free:
        k = 3 * k + v
    return base + 5 + k, base + 5 + count + k, base + 5 + 2 * count + k


def pairs():
    for x in range(BX):
        for y in range(BY):
            for z in range(BZ):
                for e in OFFSETS:
                    yield (x, y, z), e, (x + e[0], y + e[1], z + e[2])


def pad(rows, multiple, dummy):
    rows = list(rows)
    while len(rows) % multiple:
        rows.append(dummy)
    return rows


def bridge_tables():
    inner, outward, inward = [], [], [[], [], [], []]
    for t, e, b in pairs():
        own = 8 * tile_number(*t)
        s = 27 * tile_number(*t) + code(e)
        if inside(*b):
            inner.append((own, 8 * tile_number(*b), s, s, s))
        else:
            back = tuple(-v for v in e)
            outward.append((own, halo_block(*b)[0], s, s, s))
            inward[contact_class(e)].append((halo_block(*b)[0], own) + halo_slot(*b, back))
    return inner, outward, sum(inward, [])


def contact_class(e):
    kinds = sum(abs(v) for v in e)
    if kinds == 0:
        return 3
    if kinds > 1:
        return 0
    return 1 if e[0] else 2


CHUNKS = (1, 2, 4, 16)
UNROLL = (80, 16, 16, 4)


def contact_tables(halo):
    out = [[], [], [], []]
    for t, e, b in pairs():
        own = 8 * tile_number(*t)
        s = 27 * tile_number(*t) + code(e)
        back = tuple(-v for v in e)
        kind = contact_class(e)
        if inside(*b):
            s2 = 27 * tile_number(*b) + code(back)
            if not halo:
                out[kind].append((own, 8 * tile_number(*b), s, s2, s2))
        elif halo:
            _, ret, rel = halo_slot(*b, back)
            out[kind].append((own, halo_block(*b)[0], s, ret, rel))
    return out


def flat(rows):
    return np.asarray(rows, np.int32).reshape(-1)


def row(ref, at):
    return ref[pl.ds(at, 1), :]


def block(ref, at):
    return ref[pl.ds(pl.multiple_of(at, 8), 8), :]


class Listing:
    def __init__(self, count, listed, jobs):
        self.count, self.listed, self.jobs = count, listed, jobs

    def share(self, i, steps, n):
        each = -(-self.count // steps)
        assert each * steps == self.count
        for u in range(each):
            j = i * each + u
            self.jobs[n] = j
            n = n + self.listed(j)
        return n

    def close(self, n):
        for u in range(BATCH):
            self.jobs[n + u] = self.count
        return (n + BATCH - 1) // BATCH


def run_bridges(batches, jobs, tab, a_ref, b_ref, p_ref, q_ref, l_ref, scr, acc_a, acc_b, next_ref):
    m_ref, a_scr, q_scr, l_scr, f_ref, g_ref = scr

    def body(i, carry):
        at = []
        for j in range(BATCH):
            o = jobs[i * BATCH + j] * 5
            at.append([tab[o + k] for k in range(5)])
        partner = []
        for j in range(BATCH):
            a, b, p, q, l = at[j]
            idx = row(p_ref, p).astype(jnp.int32)
            m_ref[8 * j : 8 * j + 8, :] = jnp.take_along_axis(
                block(b_ref, b), jnp.broadcast_to(idx, (8, G)), axis=1
            )
            a_scr[8 * j : 8 * j + 8, :] = block(a_ref, a)
            q_scr[j : j + 1, :] = row(q_ref, q)
            l_scr[j : j + 1, :] = row(l_ref, l)
        for g in range(BATCH // 8):
            near = [m_ref[pl.ds(64 * g + c, 8, stride=8), :] for c in range(5)]
            own = [a_scr[pl.ds(64 * g + c, 8, stride=8), :] for c in range(5)]
            held = q_scr[8 * g : 8 * g + 8, :]
            half = 0.5 * l_scr[8 * g : 8 * g + 8, :]
            gap = [own[c] - near[c] for c in range(3)]
            squares = gap[0] * gap[0] + gap[1] * gap[1] + gap[2] * gap[2]
            inverse = lax.rsqrt(squares)
            spacing = squares * inverse
            radius_sum = own[3] + near[3]
            harmonic = 2.0 * own[3] * near[3] / radius_sum
            scaled = (
                jnp.maximum(spacing - radius_sum, 0.0) * harmonic * lax.rsqrt(harmonic * held)
            )
            intact = held > 0.0
            tension = harmonic * inverse / (1.0 + 1.05 * scaled + 2.5 * scaled * scaled)
            tension = jnp.where(intact, tension, 0.0)
            absorb = jnp.where(intact, ABSORB, 0.0)
            force = [tension * gap[c] for c in range(3)]
            if acc_b is not None:
                for c, value in enumerate(force + [half - absorb * near[4]]):
                    high = value.astype(jnp.bfloat16).astype(jnp.float32)
                    f_ref[pl.ds(64 * g + c, 8, stride=8), :] = high
                    f_ref[pl.ds(64 * g + 4 + c, 8, stride=8), :] = value - high
            if acc_a is not None:
                for c in range(3):
                    g_ref[pl.ds(64 * g + c, 8, stride=8), :] = -force[c]
                g_ref[pl.ds(64 * g + 3, 8, stride=8), :] = half - absorb * own[4]
                g_ref[pl.ds(64 * g + 4, 8, stride=8), :] = jnp.where(
                    intact, held + ABSORB * (own[4] + near[4]), 0.0
                )
        if acc_a is not None:
            for j in range(BATCH):
                a, b, p, q, l = at[j]
                here = pl.ds(pl.multiple_of(a, 8), 8)
                acc_a[here, :] = acc_a[here, :] + g_ref[8 * j : 8 * j + 8, :]
                next_ref[pl.ds(q, 1), :] = g_ref[8 * j + 4 : 8 * j + 5, :]
        if acc_b is not None:
            sub = lax.broadcasted_iota(jnp.int32, (G, G), 0)
            none = jnp.zeros((8, G), jnp.float32)
            for j in range(0, BATCH, 2):
                left, choose = [], []
                for h in range(2):
                    idx = row(p_ref, at[j + h][2]).astype(jnp.int32)
                    choose.append((sub == idx).astype(jnp.bfloat16))
                    value = f_ref[8 * (j + h) : 8 * (j + h) + 8, :]
                    left.append(jnp.concatenate([none] * h + [value] + [none] * (1 - h), axis=1))
                landed = lax.dot_general(
                    jnp.concatenate(left, axis=0).astype(jnp.bfloat16),
                    jnp.concatenate(choose, axis=1),
                    (((1,), (1,)), ((), ())),
                    preferred_element_type=jnp.float32,
                )
                for h in range(2):
                    here = pl.ds(pl.multiple_of(at[j + h][1], 8), 8)
                    acc_b[here, :] = acc_b[here, :] + landed[8 * h : 8 * h + 8, :]
        return carry

    lax.fori_loop(0, batches, body, 0)


def chunk_force(key, base, other, target):
    sub = lax.broadcasted_iota(jnp.int32, (8, G), 0).astype(jnp.float32) + base
    chosen = key == sub
    rows = [
        jnp.sum(jnp.where(chosen, other[c], 0.0), axis=1, keepdims=True) for c in range(4)
    ]
    radius = jnp.where(rows[3] > 0.0, rows[3], -1000.0)
    delta = [target[c] - rows[c] for c in range(3)]
    squares = delta[0] * delta[0] + delta[1] * delta[1] + delta[2] * delta[2]
    squares = jnp.maximum(squares, 1e-6)
    inverse = lax.rsqrt(squares)
    reach = target[3] + radius
    overlap = jnp.maximum(reach - squares * inverse, 0.0)
    weight = target[3] * radius * overlap
    push = overlap * inverse * weight * lax.rsqrt(jnp.maximum(weight * reach, 1e-30))
    return [push * delta[c] for c in range(3)]


def run_contacts(sizes, tab, t_ref, n_ref, q_ref, l_ref, nq_ref, nl_ref, low, high, mark, keys, seen, acc, beside=()):
    beside = dict(beside)
    lists = {}
    total = sum(sizes)
    step = max(k for k in range(1, 81) if total % k == 0)
    wide = lax.broadcasted_iota(jnp.int32, (8, G), 0)

    def near(i, carry):
        for u in range(step):
            j = i * step + u
            t, n, s, nq, nl = [tab[j * 5 + k] for k in range(5)]
            theirs = row(nq_ref, nq) + row(nl_ref, nl)
            if seen is not None:
                seen[pl.ds(j, 1), :] = theirs
            live = row(q_ref, s) + row(l_ref, s) + theirs > 0.0
            value = block(n_ref, n)
            top = block(high, t)
            gap = jnp.maximum(jnp.maximum(block(low, t) - value, value - top), 0.0)
            gap = jnp.where(wide < 3, gap * gap, 0.0)
            distance = jnp.sum(gap, axis=0, keepdims=True)
            limit = value[3:4, :] + top[3:4, :] + 0.001
            mark[pl.ds(j, 1), :] = jnp.where(
                live & (distance <= limit * limit), 1.0, 0.0
            )
        if "near" in beside:
            carry = beside["near"].share(i, total // step, carry)
        return carry

    n = lax.fori_loop(0, total // step, near, 0)
    if "near" in beside:
        lists["near"] = beside["near"].close(n)
    if "marked" in beside:
        beside["marked"]()
    lane = lax.broadcasted_iota(jnp.int32, (G, G), 1)
    sub = lax.broadcasted_iota(jnp.int32, (G, G), 0)
    upper = (sub <= lane).astype(jnp.bfloat16)
    start = 0
    crowded = []
    for kind, size in enumerate(sizes):
        if not size:
            continue
        if kind == 3:
            keys[start : start + size, :] = lax.broadcasted_iota(
                jnp.int32, (size, G), 1
            ).astype(jnp.float32)
        else:
            held = mark[start : start + size, :]
            rank = jnp.dot(
                held.astype(jnp.bfloat16), upper, preferred_element_type=jnp.float32
            )
            keys[start : start + size, :] = jnp.where(held > 0.0, rank - 1.0, -1.0)
            crowded.append((kind, start, size, jnp.max(rank) > 8.0 * CHUNKS[kind]))
        start += size

    def job(j, chunk_list):
        t, n = tab[j * 5], tab[j * 5 + 1]
        target = block(t_ref, t)
        other = block(n_ref, n)
        target = [target[c : c + 1, :] for c in range(4)]
        other = [other[c : c + 1, :] for c in range(4)]
        key = row(keys, j)
        force = None
        for base in chunk_list:
            part = chunk_force(key, base, other, target)
            force = part if force is None else [x + y for x, y in zip(force, part)]
        for c in range(3):
            here = pl.ds(pl.multiple_of(t * 3 + 8 * c, 8), 8)
            acc[here, :] = acc[here, :] + force[c]

    start = 0
    for kind, size in enumerate(sizes):
        if not size:
            continue
        unroll = UNROLL[kind]

        def body(i, carry, start=start, kind=kind, unroll=unroll):
            for u in range(unroll):
                job(start + i * unroll + u, [8.0 * c for c in range(CHUNKS[kind])])
            if kind in beside:
                carry = beside[kind].share(i, size // unroll, carry)
            return carry

        if kind in beside and "ready" in beside:
            beside["ready"]()
        n = lax.fori_loop(0, size // unroll, body, 0)
        if kind in beside:
            lists[kind] = beside[kind].close(n)
        start += size

    for kind, start, size, over in crowded:

        @pl.when(over)
        def _(kind=kind, start=start, size=size):
            def rest(j, carry):
                def one(c, inner):
                    job(start + j, [8.0 * c.astype(jnp.float32)])
                    return inner

                return lax.fori_loop(CHUNKS[kind], 16, one, carry)

            lax.fori_loop(0, size, rest, 0)

    return lists


def bounds(st_ref, low, high):
    for t in range(TILES):
        value = st_ref[8 * t : 8 * t + 8, :]
        low[8 * t : 8 * t + 8, :] = jnp.broadcast_to(
            jnp.min(value, axis=1, keepdims=True), (8, G)
        )
        high[8 * t : 8 * t + 8, :] = jnp.broadcast_to(
            jnp.max(value, axis=1, keepdims=True), (8, G)
        )


def settle(acc):
    rows = []
    for t in range(TILES):
        for c in range(3):
            at = 24 * t + 8 * c
            rows.append(jnp.sum(acc[at : at + 8, :], axis=0, keepdims=True))
    return rows


def first_kernel(sizes, tab_c, st, ret, rel, after, low, high, acc, mark, keys):
    acc[...] = jnp.zeros_like(acc)
    bounds(st, low, high)
    run_contacts(sizes, tab_c, st, st, ret, rel, ret, rel, low, high, mark, keys, None, acc)


def bridge_kernel(
    sizes, count, tab_c, tab_b, live, st, part, ret, rel, low, high, before, after,
    acc, acc_a, fresh, *scr
):
    *bridge, acc_b, mark, keys, jobs = scr
    acc[...] = before[...]
    acc_a[...] = jnp.zeros_like(acc_a)
    acc_b[...] = jnp.zeros_like(acc_b)
    fresh[...] = jnp.zeros_like(fresh)
    listing = Listing(count, lambda j: live[tab_b[j * 5 + 2]], jobs)
    lists = run_contacts(
        sizes, tab_c, st, st, ret, rel, ret, rel, low, high, mark, keys, None, acc,
        beside={3: listing},
    )
    run_bridges(lists[3], jobs, tab_b, st, st, part, ret, rel, bridge, acc_a, acc_b, fresh)
    for t in range(TILES):
        at = 8 * t
        acc_a[at : at + 4, :] = (
            acc_a[at : at + 4, :] + acc_b[at : at + 4, :] + acc_b[at + 4 : at + 8, :]
        )


def third_kernel(sizes, tab_c, st, ret, rel, low, high, before, after, acc, mark, keys):
    acc[...] = before[...]
    run_contacts(sizes, tab_c, st, st, ret, rel, ret, rel, low, high, mark, keys, None, acc)


def halo_kernel(
    sizes, n_out, n_in, tab_o, tab_i, tab_c, live, st, part, ret, rel, low, high, held, pushed,
    before, za, zb, ya, yb, xa, xb, forces, film, fresh, *scr
):
    (*bridge, acc_a, acc_b, mark, keys, seen, acc, halo, store, flag, jobs_o, jobs_i, flags, sems) = scr
    copies = []
    for k, (pair, axis, at, rows) in enumerate(
        (((za, zb), "gz", Z_AT, Z_ROWS), ((ya, yb), "gy", Y_AT, Y_ROWS), ((xa, xb), "gx", X_AT, X_ROWS))
    ):
        odd = lax.axis_index(axis) % 2
        for w, src in enumerate(pair):
            side = (1 - odd) if w == 0 else odd
            copy = pltpu.make_async_copy(
                src, halo.at[pl.ds(at + side * rows, rows), :], sems.at[2 * k + w]
            )
            copy.start()
            copies.append(copy)
    keep = pltpu.make_async_copy(before, store, sems.at[6])
    keep.start()
    acc_a[...] = held[...]
    acc_b[...] = jnp.zeros_like(acc_b)
    acc[...] = pushed[...]
    halo[ZERO_AT : ZERO_AT + 8, :] = jnp.zeros((8, G), jnp.float32)
    seen[sum(sizes) :, :] = jnp.zeros((512 - sum(sizes), G), jnp.float32)
    for copy in copies:
        copy.wait()
    down = pltpu.make_async_copy(flag, flags, sems.at[7])

    def marked():
        first = (
            lax.broadcasted_iota(jnp.int32, (8, G), 0) + lax.broadcasted_iota(jnp.int32, (8, G), 1)
        ) == 0
        listed = lax.dot_general(
            first.astype(jnp.bfloat16),
            (seen[...] > 0.0).astype(jnp.bfloat16),
            (((1,), (1,)), ((), ())),
            preferred_element_type=jnp.float32,
        )
        for k in range(4):
            flag[k : k + 1, :] = listed[0:1, k * G : k * G + G].astype(jnp.int32)
        down.start()

    lists = run_contacts(
        sizes, tab_c, st, halo, ret, rel, halo, halo, low, high, mark, keys, seen, acc,
        beside={
            "near": Listing(n_out, lambda j: live[tab_o[j * 5 + 2]], jobs_o),
            "marked": marked,
            "ready": down.wait,
            0: Listing(n_in, lambda j: flags[j // G, j % G], jobs_i),
        },
    )
    keep.wait()
    run_bridges(lists["near"], jobs_o, tab_o, st, halo, part, ret, rel, bridge, acc_a, None, store)
    leave = pltpu.make_async_copy(store.at[pl.ds(0, SLOTS), :], fresh, sems.at[6])
    leave.start()
    run_bridges(lists[0], jobs_i, tab_i, halo, st, halo, halo, halo, bridge, None, acc_b, None)
    rows = settle(acc)
    for t in range(TILES):
        at = 8 * t
        value = acc_a[at : at + 4, :] + acc_b[at : at + 4, :] + acc_b[at + 4 : at + 8, :]
        for c in range(3):
            forces[c, t : t + 1, :] = value[c : c + 1, :] + rows[3 * t + c]
        film[t : t + 1, :] = value[3:4, :] + st[at + 4 : at + 5, :]
    leave.wait()


def send_sides(axis):
    odd = lax.axis_index(axis) % 2
    return 1 - odd, odd


def own_slots(refs, at):
    return [ref[pl.ds(at, 9), :].astype(jnp.float32) for ref in refs]


def pack_z_kernel(
    pos_in, rad_in, film_in, live_in, part_in, broken_in, vol_in, st, part, ret, rel, out_a, out_b,
    pos, rad, film, live, broken, vol, sems,
):
    copies = [
        pltpu.make_async_copy(src, dst, sems.at[k])
        for k, (src, dst) in enumerate(
            (
                (live_in, live), (broken_in, broken), (vol_in, vol), (part_in, part),
                (pos_in, pos), (rad_in, rad), (film_in, film),
            )
        )
    ]
    for copy in copies:
        copy.start()
    for copy in copies:
        copy.wait()
    flags = [live[0:1, G * k : G * k + G] for k in range(SLOTS // G)]
    rest = SLOTS - G * (SLOTS // G)
    flags.append(
        jnp.concatenate(
            [live[0:1, SLOTS - rest : SLOTS], jnp.zeros((1, G - rest), jnp.int32)], axis=1
        )
    )
    flags.append(jnp.zeros((8 - len(flags), G), jnp.int32))
    columns = jnp.transpose(jnp.concatenate(flags, axis=0).astype(jnp.float32))
    for k in range(SLOTS // G + 1):
        count = min(G, SLOTS - G * k)
        here = slice(G * k, G * k + count)
        listed = jnp.broadcast_to(columns[0:count, k : k + 1], (count, G)) > 0.0
        lost = broken[here, :] > 0
        held = jnp.where(listed, vol[here, :], 0.0)
        ret[here, :] = jnp.where(lost, 0.0, held)
        rel[here, :] = jnp.where(lost, held, 0.0)
    for ref in (ret, rel):
        ref[SLOTS : SLOTS + 8, :] = jnp.zeros((8, G), jnp.float32)
    for g in range(TILES // 8):
        members = [pos[c, 8 * g : 8 * g + 8, :] for c in range(3)]
        members += [rad[8 * g : 8 * g + 8, :], film[8 * g : 8 * g + 8, :]]
        for c, value in enumerate(members):
            st[pl.ds(64 * g + c, 8, stride=8), :] = value
        for c in range(5, 8):
            st[pl.ds(64 * g + c, 8, stride=8), :] = jnp.zeros((8, G), jnp.float32)
    for out, side in zip((out_a, out_b), send_sides("gz")):
        for xy in range(16):
            t = 2 * xy + side
            at = 32 * xy
            out[at : at + 5, :] = st[pl.ds(8 * t, 5), :]
            for k, ref in enumerate((part, ret, rel)):
                rows = ref[pl.ds(27 * t + 2 * side, 9, stride=3), :]
                out[at + 5 + 9 * k : at + 14 + 9 * k, :] = rows.astype(jnp.float32)


def load_sides(pair, axis, buf, rows, sems, first):
    odd = lax.axis_index(axis) % 2
    copies = []
    for w, src in enumerate(pair):
        side = (1 - odd) if w == 0 else odd
        copy = pltpu.make_async_copy(src, buf.at[pl.ds(side * rows, rows), :], sems.at[first + w])
        copy.start()
        copies.append(copy)
    return copies


def pack_y_kernel(st, part, ret, rel, za, zb, after, out_a, out_b, zbuf, sems):
    for copy in load_sides((za, zb), "gz", zbuf, Z_ROWS, sems, 0):
        copy.wait()
    for out, side in zip((out_a, out_b), send_sides("gy")):
        for x in range(4):
            for z in range(2):
                t = tile_number(x, 3 * side, z)
                at = 32 * (2 * x + z)
                out[at : at + 5, :] = st[pl.ds(8 * t, 5), :]
                for k, ref in enumerate((part, ret, rel)):
                    for i in range(3):
                        here = at + 5 + 9 * k + 3 * i
                        rows = ref[pl.ds(27 * t + 9 * i + 6 * side, 3), :]
                        out[here : here + 3, :] = rows.astype(jnp.float32)
        for sz in range(2):
            for x in range(4):
                at = 256 + 16 * (4 * sz + x)
                src = sz * Z_ROWS + (x * 4 + 3 * side) * 32
                out[at : at + 5, :] = zbuf[pl.ds(src, 5), :]
                for k in range(3):
                    out[at + 5 + 3 * k : at + 8 + 3 * k, :] = zbuf[
                        pl.ds(src + 5 + 9 * k + 2 * side, 3, stride=3), :
                    ]
                out[at + 14 : at + 16, :] = jnp.zeros((2, G), jnp.float32)


def pack_x_kernel(st, part, ret, rel, za, zb, ya, yb, after, out_a, out_b, zbuf, ybuf, sems):
    copies = load_sides((za, zb), "gz", zbuf, Z_ROWS, sems, 0)
    copies += load_sides((ya, yb), "gy", ybuf, Y_ROWS, sems, 2)
    for copy in copies:
        copy.wait()
    for out, side in zip((out_a, out_b), send_sides("gx")):
        for y in range(4):
            for z in range(2):
                t = tile_number(3 * side, y, z)
                at = 32 * (2 * y + z)
                out[at : at + 5, :] = st[pl.ds(8 * t, 5), :]
                for k, ref in enumerate((part, ret, rel)):
                    rows = ref[pl.ds(27 * t + 18 * side, 9), :]
                    out[at + 5 + 9 * k : at + 14 + 9 * k, :] = rows.astype(jnp.float32)
        for sy in range(2):
            for z in range(2):
                at = 256 + 16 * (2 * sy + z)
                src = sy * Y_ROWS + (2 * 3 * side + z) * 32
                out[at : at + 5, :] = ybuf[pl.ds(src, 5), :]
                for k in range(3):
                    out[at + 5 + 3 * k : at + 8 + 3 * k, :] = ybuf[
                        pl.ds(src + 5 + 9 * k + 6 * side, 3), :
                    ]
                out[at + 14 : at + 16, :] = jnp.zeros((2, G), jnp.float32)
        for sz in range(2):
            for y in range(4):
                at = 320 + 16 * (4 * sz + y)
                src = sz * Z_ROWS + (4 * 3 * side + y) * 32
                out[at : at + 5, :] = zbuf[pl.ds(src, 5), :]
                for k in range(3):
                    out[at + 5 + 3 * k : at + 8 + 3 * k, :] = zbuf[
                        pl.ds(src + 5 + 9 * k + 6 * side, 3), :
                    ]
                out[at + 14 : at + 16, :] = jnp.zeros((2, G), jnp.float32)
        for sy in range(2):
            for sz in range(2):
                at = 448 + 8 * (2 * sy + sz)
                src = sy * Y_ROWS + 256 + 16 * (4 * sz + 3 * side)
                out[at : at + 5, :] = ybuf[pl.ds(src, 5), :]
                for k in range(3):
                    out[at + 5 + k : at + 6 + k, :] = ybuf[
                        pl.ds(src + 5 + 3 * k + 2 * side, 1), :
                    ]


VM = pl.BlockSpec(memory_space=pltpu.VMEM)
SM = pl.BlockSpec(memory_space=pltpu.SMEM)
AN = pl.BlockSpec(memory_space=pl.ANY)
PARAMS = pltpu.CompilerParams(vmem_limit_bytes=48 * 1024 * 1024)


def rows_of(n):
    return jax.ShapeDtypeStruct((n, G), jnp.float32)


def swap(pair, axis):
    count = lax.axis_size(axis)
    first, second = pair
    near = [(i, i ^ 1) for i in range(count) if i ^ 1 < count]
    far = [(i, ((i + 1) ^ 1) - 1) for i in range(1, count) if ((i + 1) ^ 1) - 1 < count]
    return lax.ppermute(first, axis, near), lax.ppermute(second, axis, far)


def bridge_scratch():
    return [
        pltpu.VMEM((8 * BATCH, G), jnp.float32),
        pltpu.VMEM((8 * BATCH, G), jnp.float32),
        pltpu.VMEM((BATCH, G), jnp.float32),
        pltpu.VMEM((BATCH, G), jnp.float32),
        pltpu.VMEM((8 * BATCH, G), jnp.float32),
        pltpu.VMEM((8 * BATCH, G), jnp.float32),
    ]


def tiles_scratch(count):
    return [pltpu.VMEM((8 * TILES, G), jnp.float32)] * count


def contact_scratch(jobs):
    return [pltpu.VMEM((jobs, G), jnp.float32)] * 2


def shards(positions, grain_radii, film_liquid, pair_live, partner, rupture, volume):
    pos = positions.reshape(3, TILES, G)
    rad = grain_radii.reshape(TILES, G)
    film = film_liquid.reshape(TILES, G)
    part = partner.reshape(SLOTS, G)
    vol = volume.reshape(SLOTS, G)
    broken = rupture.reshape(SLOTS, G)

    st, part, ret, rel, za, zb = pl.pallas_call(
        pack_z_kernel,
        out_shape=(
            rows_of(8 * TILES),
            jax.ShapeDtypeStruct((SLOTS, G), jnp.int32),
            rows_of(SLOTS + 8),
            rows_of(SLOTS + 8),
            rows_of(Z_ROWS),
            rows_of(Z_ROWS),
        ),
        in_specs=[pl.BlockSpec(memory_space=pltpu.HBM)] * 7,
        out_specs=(VM,) * 6,
        scratch_shapes=[
            pltpu.VMEM((3, TILES, G), jnp.float32),
            pltpu.VMEM((TILES, G), jnp.float32),
            pltpu.VMEM((TILES, G), jnp.float32),
            pltpu.VMEM((1, SLOTS), jnp.int32),
            pltpu.VMEM((SLOTS, G), jnp.int32),
            pltpu.VMEM((SLOTS, G), jnp.float32),
            pltpu.SemaphoreType.DMA((7,)),
        ],
        compiler_params=PARAMS,
        name="pack_z",
    )(
        *[
            pltpu.with_memory_space_constraint(value, pltpu.HBM)
            for value in (pos, rad, film, pair_live.reshape(1, SLOTS), part, broken, vol)
        ]
    )
    zero = SLOTS
    flags = pair_live.reshape(SLOTS)

    def near_jobs(kinds):
        near = contact_tables(False)
        near = [
            pad(near[k], UNROLL[k], (0, 0, zero, zero, zero)) if k in kinds else [] for k in range(4)
        ]
        return tuple(len(rows) for rows in near), flat(sum(near, []))

    inner, outward, inward = bridge_tables()
    dummy = (0, 0, 0, zero, zero)
    sums = rows_of(24 * TILES)
    tile_rows = rows_of(8 * TILES)
    za, zb = swap((za, zb), "gz")
    sizes, tab = near_jobs((0, 1))
    low, high, pushed = pl.pallas_call(
        functools.partial(first_kernel, sizes),
        out_shape=(tile_rows, tile_rows, sums),
        in_specs=[SM] + [VM] * 3 + [AN],
        out_specs=(VM,) * 3,
        scratch_shapes=contact_scratch(sum(sizes)),
        compiler_params=PARAMS,
        name="first",
    )(tab, st, ret, rel, st)
    ya, yb = pl.pallas_call(
        pack_y_kernel,
        out_shape=(rows_of(Y_ROWS),) * 2,
        in_specs=[VM] * 4 + [AN] * 3,
        out_specs=(VM,) * 2,
        scratch_shapes=[pltpu.VMEM((2 * Z_ROWS, G), jnp.float32), pltpu.SemaphoreType.DMA((2,))],
        compiler_params=PARAMS,
        name="pack_y",
    )(st, part, ret, rel, za, zb, pushed)
    order_y = ya
    ya, yb = swap((ya, yb), "gy")
    sizes, tab = near_jobs((3,))
    pushed, held, fresh = pl.pallas_call(
        functools.partial(bridge_kernel, sizes, len(inner)),
        out_shape=(sums, tile_rows, rows_of(SLOTS + 8)),
        in_specs=[SM] * 3 + [VM] * 7 + [AN],
        out_specs=(VM,) * 3,
        scratch_shapes=bridge_scratch()
        + tiles_scratch(1)
        + contact_scratch(sum(sizes))
        + [pltpu.SMEM((len(inner) + BATCH,), jnp.int32)],
        compiler_params=PARAMS,
        name="bridge_own",
    )(tab, flat(inner + [dummy]), flags, st, part, ret, rel, low, high, pushed, order_y)
    xa, xb = pl.pallas_call(
        pack_x_kernel,
        out_shape=(rows_of(X_ROWS),) * 2,
        in_specs=[VM] * 4 + [AN] * 5,
        out_specs=(VM,) * 2,
        scratch_shapes=[
            pltpu.VMEM((2 * Z_ROWS, G), jnp.float32),
            pltpu.VMEM((2 * Y_ROWS, G), jnp.float32),
            pltpu.SemaphoreType.DMA((4,)),
        ],
        compiler_params=PARAMS,
        name="pack_x",
    )(st, part, ret, rel, za, zb, ya, yb, held)
    order_x = xa
    xa, xb = swap((xa, xb), "gx")
    sizes, tab = near_jobs((2,))
    pushed = pl.pallas_call(
        functools.partial(third_kernel, sizes),
        out_shape=sums,
        in_specs=[SM] + [VM] * 6 + [AN],
        out_specs=VM,
        scratch_shapes=contact_scratch(sum(sizes)),
        compiler_params=PARAMS,
        name="third",
    )(tab, st, ret, rel, low, high, pushed, order_x)

    far = contact_tables(True)
    far = [pad(rows, UNROLL[k], (0, 0, zero, ZERO_AT, ZERO_AT)) for k, rows in enumerate(far)]
    sizes = tuple(len(rows) for rows in far)
    inward = pad(inward, 5, (0, 0, ZERO_AT, ZERO_AT, ZERO_AT))
    forces, film_next, fresh = pl.pallas_call(
        functools.partial(halo_kernel, sizes, len(outward), len(inward)),
        out_shape=(
            jax.ShapeDtypeStruct((3, TILES, G), jnp.float32),
            rows_of(TILES),
            rows_of(SLOTS),
        ),
        in_specs=[SM] * 4 + [VM] * 8 + [AN] * 7,
        out_specs=(VM, VM, AN),
        scratch_shapes=bridge_scratch()
        + tiles_scratch(2)
        + contact_scratch(sum(sizes))
        + [
            pltpu.VMEM((512, G), jnp.float32),
            pltpu.VMEM((24 * TILES, G), jnp.float32),
            pltpu.VMEM((HALO_ROWS, G), jnp.float32),
            pltpu.VMEM((SLOTS + 8, G), jnp.float32),
            pltpu.VMEM((8, G), jnp.int32),
            pltpu.SMEM((len(outward) + BATCH,), jnp.int32),
            pltpu.SMEM((len(inward) + BATCH,), jnp.int32),
            pltpu.SMEM((8, G), jnp.int32),
            pltpu.SemaphoreType.DMA((8,)),
        ],
        compiler_params=PARAMS,
        name="halo",
    )(
        flat(outward + [dummy]),
        flat(inward + [(0, 0, ZERO_AT, ZERO_AT, ZERO_AT)]),
        flat(sum(far, [])),
        flags, st, part, ret, rel, low, high, held, pushed, fresh,
        za, zb, ya, yb, xa, xb,
    )
    return (
        forces.reshape(positions.shape),
        film_next.reshape(film_liquid.shape),
        fresh.reshape(volume.shape),
    )


def solution(mesh):
    return jax.shard_map(
        shards,
        mesh=mesh,
        in_specs=(
            P(None, "gx", "gy", "gz", None),
            P("gx", "gy", "gz", None),
            P("gx", "gy", "gz", None),
            P("gx", "gy", "gz", None),
            P("gx", "gy", "gz", None, None),
            P("gx", "gy", "gz", None, None),
            P("gx", "gy", "gz", None, None),
        ),
        out_specs=(
            P(None, "gx", "gy", "gz", None),
            P("gx", "gy", "gz", None),
            P("gx", "gy", "gz", None, None),
        ),
        check_vma=False,
    )
```
